32 devices in a mesh: layer: 4 (over y, x), expert: 4 (over z), dp: 2 (over core).
Axes of the slice: x: 2, y: 2, z: 4, core: 2. Of those that a mesh axis runs over, the one named last changes fastest.
Arguments:
- tokens: bfloat16 [2048, 2304], P(('expert', 'dp')), may hold values from -6 to 6
- expert_ids: int32 [2048], P(('expert', 'dp')), may hold values from 0 to 3, as said below
- slot_ids: int32 [2048], P(('expert', 'dp')), may hold values from 0 to 127, as said below
- live_mask: int32 [2048], P(('expert', 'dp')), may hold values from 0 to 1
- w_enc: bfloat16 [4, 2304, 2048], P('expert', None, 'layer'), may hold values from -0.125 to 0.125
- b_enc: float32 [4, 2048], P('expert', 'layer'), may hold values from -3 to 3
- w_dec: bfloat16 [2, 4, 2048, 2304], P(None, 'expert', 'layer'), may hold values from -0.125 to 0.125
- b_dec: float32 [2, 2304], P(None, 'layer'), may hold values from -3 to 3
- targets: bfloat16 [2, 2048, 2304], P(None, ('expert', 'dp'), 'layer'), may hold values from -6 to 6
Outputs:
- recon: bfloat16 [2, 2048, 2304], P(None, ('expert', 'dp'), 'layer')
- grad_w_enc: bfloat16 [4, 2304, 2048], P('expert', 'dp', 'layer')
- grad_b_enc: float32 [4, 2048], P('expert', ('layer', 'dp'))
- grad_w_dec: bfloat16 [2, 4, 2048, 2304], P(None, 'expert', 'layer', 'dp')
- grad_b_dec: float32 [2, 2304], P(None, 'layer')
The draws below stay inside these ranges and needn't reach their ends.
Inputs may be any that keep to these rules, and one draw needn't show every extreme that they name: `expert_ids`: the 256 tokens of one block name any expert at most 128 times; in every draw one expert is named exactly 128 times by every block. `slot_ids`: tokens of one block that name the same expert have distinct slots.
All inputs are finite; a program needn't handle non-finite values.
Results may differ from the reference program's by a relative error of at most 0.01.
Values may be sent and summed in bfloat16 or wider, within the bound.
A program may use at most 128 MiB of HBM per device.

```python
import math
import jax
import jax.numpy as jnp
from jax import lax

D = 2304
LAT = 2048
TGT = 2
TOK_DEV = 256
EXPERTS = 4
BLOCKS = 8
TOKENS = 2048
CAP = 128
N_LAYER = 4


def route_cells(key):
    base = jax.random.fold_in(key, 7301)
    busiest = jax.random.randint(jax.random.fold_in(base, 1), (), 0, EXPERTS)
    block_keys = jax.random.split(jax.random.fold_in(base, 2), BLOCKS)
    total_cells = EXPERTS * CAP

    def one_block(block_key):
        key_order, key_second, key_tokens = jax.random.split(block_key, 3)
        cell_ids = jnp.arange(total_cells, dtype=jnp.int32)
        owner_id = cell_ids // CAP
        second = jax.random.randint(key_second, (), 0, EXPERTS)
        tier_rank = jnp.where(owner_id == busiest, 0, jnp.where(owner_id == second, 1, 2)).astype(jnp.int32)
        cell_rank = jnp.argsort(jax.random.permutation(key_order, total_cells)).astype(jnp.int32)
        cell_order = jnp.argsort(tier_rank * total_cells + cell_rank).astype(jnp.int32)
        chosen = cell_order[:TOK_DEV]
        shuffled = chosen[jax.random.permutation(key_tokens, TOK_DEV)]
        return (shuffled // CAP, shuffled % CAP)
    experts_all, slots_all = jax.vmap(one_block)(block_keys)
    return (experts_all.reshape(TOKENS).astype(jnp.int32), slots_all.reshape(TOKENS).astype(jnp.int32))


def draw_expert_ids(key, part):
    return route_cells(key)[0]


def draw_slot_ids(key, part):
    return route_cells(key)[1]


def draw_live_mask(key, part):
    lengths = jax.random.randint(jax.random.fold_in(key, 9157), (BLOCKS,), TOK_DEV // 4, TOK_DEV + 1)
    positions = jnp.arange(TOK_DEV, dtype=jnp.int32)
    return (positions[None, :] < lengths[:, None]).astype(jnp.int32).reshape(TOKENS)


def level_of(rng, dims, cuts, low, high):
    factor_of = 1.0
    for position, parts in cuts:
        heights = jax.random.uniform(jax.random.fold_in(jax.random.fold_in(rng, 6), position), (parts,), jnp.float32, low / len(cuts), high / len(cuts))
        factor_of = factor_of * jnp.repeat(jnp.exp(heights), dims[position] // parts).reshape((-1,) + (1,) * (len(dims) - 1 - position))
    return factor_of


def centred(rng, extent, width, limit, cuts=(), kind=jnp.bfloat16):
    array = width * jax.random.normal(rng, extent, jnp.float32)
    if cuts:
        array = array * level_of(rng, extent, cuts, -0.22, 0.18)
    return jnp.clip(array, -limit, limit).astype(kind)


def setup_inputs(seed: int = 0) -> dict:
    key_list = jax.random.split(jax.random.key(seed), 10)
    tokens = centred(key_list[0], (TOKENS, D), 1.0, 6.0, ((0, 8),))
    expert_ids = draw_expert_ids(jax.random.fold_in(key_list[9], 71), 0)
    slot_ids = draw_slot_ids(jax.random.fold_in(key_list[9], 71), 0)
    live_mask = draw_live_mask(jax.random.fold_in(key_list[9], 71), 0)
    w_enc = centred(key_list[4], (EXPERTS, D, LAT), D ** -0.5, 0.125, ((0, 4), (2, 4)))
    b_enc = centred(key_list[5], (EXPERTS, LAT), 0.5, 3.0, ((0, 4), (1, 4)), jnp.float32)
    w_dec = centred(key_list[6], (TGT, EXPERTS, LAT, D), LAT ** -0.5, 0.125, ((1, 4), (2, 4)))
    b_dec = centred(key_list[7], (TGT, D), 0.5, 3.0, ((1, 4),), jnp.float32)
    targets = centred(key_list[8], (TGT, TOKENS, D), 1.0, 6.0, ((1, 8), (2, 4)))
    return dict(tokens=tokens, expert_ids=expert_ids, slot_ids=slot_ids, live_mask=live_mask, w_enc=w_enc, b_enc=b_enc, w_dec=w_dec, b_dec=b_dec, targets=targets)


def reference(tokens, expert_ids, slot_ids, live_mask, w_enc, b_enc, w_dec, b_dec, targets):
    coef = 2.0 / math.sqrt(TOK_DEV)
    rows_expert = BLOCKS * CAP
    quarter = LAT // N_LAYER
    token_ids = jnp.arange(TOKENS, dtype=jnp.int32)
    row_ids = (token_ids // TOK_DEV * CAP + slot_ids).astype(jnp.int32)
    row_table = jnp.full((EXPERTS, rows_expert), TOKENS, jnp.int32).at[expert_ids, row_ids].set(token_ids)
    tokens_pad = jnp.concatenate([tokens, jnp.zeros((1, D), tokens.dtype)], axis=0)
    targets_pad = jnp.concatenate([targets, jnp.zeros((TGT, 1, D), targets.dtype)], axis=1)
    live_pad = jnp.concatenate([live_mask, jnp.zeros((1,), jnp.int32)]).astype(jnp.float32)

    def one_expert(carry_state, expert):
        recon_out, bias_total = carry_state
        expert_rows = row_table[expert]
        inputs = tokens_pad[expert_rows]
        pre_act = jnp.dot(inputs, w_enc[expert], preferred_element_type=jnp.float32) + b_enc[expert][None, :]
        active = jnp.maximum(pre_act, 0.0)
        latents = (active * active).astype(jnp.bfloat16)
        rebuilt = []
        for target in range(TGT):
            summed = jnp.zeros((rows_expert, D), jnp.float32)
            for quarter_id in range(N_LAYER):
                first = quarter_id * quarter
                partial_value = jnp.dot(latents[:, first:first + quarter], w_dec[target, expert, first:first + quarter], preferred_element_type=jnp.float32).astype(jnp.bfloat16)
                summed = summed + lax.optimization_barrier(partial_value).astype(jnp.float32)
            rebuilt.append(summed.astype(jnp.bfloat16))
        recon_sum = jnp.stack(rebuilt)
        recon_full = lax.optimization_barrier(recon_sum).astype(jnp.float32) + b_dec[:, None, :]
        recon_rows = recon_full.astype(jnp.bfloat16)
        wanted = targets_pad[:, expert_rows].astype(jnp.float32)
        live_rows = live_pad[expert_rows]
        error_grad = (coef * live_rows[None, :, None] * (recon_full - wanted)).astype(jnp.bfloat16)
        error_wide = lax.optimization_barrier(error_grad).astype(jnp.float32)
        bias_total = bias_total + lax.optimization_barrier(jnp.sum(error_wide, axis=1))
        latent_wide = latents.astype(jnp.float32)
        grad_dec = jnp.einsum('rl,trd->tld', latent_wide, error_wide)
        grad_latent = jnp.einsum('trd,tld->rl', error_wide, w_dec[:, expert].astype(jnp.float32))
        grad_pre = (grad_latent * (2.0 * active)).astype(jnp.bfloat16)
        grad_wide = lax.optimization_barrier(grad_pre).astype(jnp.float32)
        grad_enc = jnp.einsum('rd,rl->dl', inputs.astype(jnp.float32), grad_wide)
        grad_bias = lax.optimization_barrier(jnp.sum(grad_wide, axis=0))
        recon_out = recon_out.at[:, expert_rows].set(recon_rows)
        return ((recon_out, bias_total), (grad_enc.astype(jnp.bfloat16), grad_bias, grad_dec.astype(jnp.bfloat16)))
    initial = (jnp.zeros((TGT, TOKENS + 1, D), jnp.bfloat16), jnp.zeros((TGT, D), jnp.float32))
    (recon_out, bias_total), (grad_w_enc, grad_b_enc, grad_stack) = lax.scan(one_expert, initial, jnp.arange(EXPERTS, dtype=jnp.int32))
    grad_w_dec = jnp.swapaxes(grad_stack, 0, 1)
    return (recon_out[:, :TOKENS], grad_w_enc, grad_b_enc, grad_w_dec, bias_total)
```

```python
import functools
import math

import jax
import jax.numpy as jnp
from jax import lax
from jax.experimental import pallas as pl
from jax.experimental.pallas import tpu as pltpu
from jax.sharding import PartitionSpec as P


def swap(values, mask, axis="layer"):
    size = lax.axis_size(axis)
    return lax.ppermute(values, axis, [(i, i ^ mask) for i in range(size)])


def exchange_experts(values):
    size = lax.axis_size("expert")
    if size != 4:
        return lax.all_to_all(values, "expert", split_axis=1, concat_axis=1, tiled=True)
    width = values.shape[1] // size
    blocks = [values[:, k * width : (k + 1) * width] for k in range(size)]
    for mask in (2, 3, 1):
        blocks[mask] = swap(blocks[mask], mask, "expert")
    return jnp.concatenate(blocks, axis=1)


def sum_all(values, axes):
    for axis in axes:
        size = lax.axis_size(axis)
        if size & (size - 1):
            values = lax.psum(values, axis)
            continue
        mask = 1
        while mask < size:
            values = values + swap(values, mask, axis)
            mask *= 2
    return values


def share_sum(product, rows, fills):
    depth = rows.shape[0] // 2
    me = lax.axis_index("dp")
    sent = product(lax.dynamic_slice_in_dim(rows, (1 - me) * depth, depth, 0))
    came = swap(sent.astype(fills), 1, "dp")
    own = product(lax.dynamic_slice_in_dim(rows, me * depth, depth, 0))
    return own + came.astype(jnp.float32)


def gather_layers(piece, beside=None):
    size = lax.axis_size("layer")
    if size != 4 or piece.shape[0] % 2:
        return lax.all_gather(piece, "layer", axis=0, tiled=True), beside
    me = lax.axis_index("layer")
    depth = piece.shape[0]
    half = depth // 2
    near = swap(piece, 1)
    far = swap(piece, 2)
    if beside is not None:
        near, far, beside = lax.optimization_barrier((near, far, beside))
    first = swap(far[:half], 1)
    second = swap(near[half:], 2)
    whole = jnp.zeros((size * depth,) + piece.shape[1:], piece.dtype)
    for offset, value in (
        (me * depth, piece),
        ((me ^ 1) * depth, near),
        ((me ^ 2) * depth, far),
        ((me ^ 3) * depth, first),
        ((me ^ 3) * depth + half, second),
    ):
        whole = lax.dynamic_update_slice_in_dim(whole, value, offset, 0)
    return whole, beside


def scatter_sum(values):
    size = lax.axis_size("layer")
    depth = values.shape[0] // size
    if size != 4 or depth % 2:
        return lax.psum_scatter(values, "layer", scatter_dimension=0, tiled=True)
    f32 = jnp.float32
    me = lax.axis_index("layer")
    low, high = me % 2, me // 2
    pieces = values.reshape((2, 2, 2, depth // 2) + values.shape[1:])

    def pick(array, index, axis):
        return lax.dynamic_index_in_dim(array, index, axis, keepdims=False)

    one, two = pieces[:, :, 0], pieces[:, :, 1]
    one_in = swap(pick(one, 1 - low, 1), 1)
    two_in = swap(pick(two, 1 - high, 0), 2)
    one_sum = pick(one, low, 1).astype(f32) + one_in.astype(f32)
    two_sum = pick(two, high, 0).astype(f32) + two_in.astype(f32)
    one_last = swap(pick(one_sum, 1 - high, 0).astype(values.dtype), 2)
    two_last = swap(pick(two_sum, 1 - low, 0).astype(values.dtype), 1)
    return jnp.concatenate(
        [
            (pick(one_sum, high, 0) + one_last.astype(f32)).astype(values.dtype),
            (pick(two_sum, low, 0) + two_last.astype(f32)).astype(values.dtype),
        ]
    )


def plain(tokens, expert_ids, slot_ids, live_mask, w_enc, b_enc, w_dec, b_dec, targets):
    f32, bf16 = jnp.float32, jnp.bfloat16
    n_expert = lax.axis_size("expert")
    n_layer = lax.axis_size("layer")
    assert lax.axis_size("dp") == 2
    tok_rows, model_width = tokens.shape
    capacity = 2 * tok_rows // n_expert
    total_cells = n_expert * capacity
    offset = lax.axis_index("expert") if n_expert == 4 else 0
    cell_index = (expert_ids ^ offset) * capacity + slot_ids
    quarter = model_width // n_layer
    targets_count = w_dec.shape[0]
    enc_weight = w_enc[0]
    place = (
        lax.broadcasted_iota(jnp.int32, (total_cells, tok_rows), 0) == cell_index[None, :]
    ).astype(bf16)

    cells = lax.dot_general(
        tokens, place, (((0,), (1,)), ((), ())), preferred_element_type=f32
    ).astype(bf16)
    own = lax.dynamic_slice_in_dim(cells, lax.axis_index("layer") * quarter, quarter, 0)
    arrived_part = exchange_experts(own)
    arrived, _ = gather_layers(arrived_part)
    pre_act = jnp.einsum("dr,dl->rl", arrived, enc_weight, preferred_element_type=f32)
    pre_act = pre_act + b_enc[0][None, :]
    active = jnp.maximum(pre_act, 0.0)
    latents = (active * active).astype(bf16)

    coef = 2.0 / math.sqrt(tok_rows)
    live_wide = live_mask.astype(f32)
    partials = [
        jnp.einsum("ld,rl->dr", w_dec[t, 0], latents, preferred_element_type=f32).astype(bf16)
        for t in range(targets_count)
    ]
    summed = [scatter_sum(p) for p in partials]
    recons, errors, parts = [], [], []
    for t in range(targets_count):
        returned = exchange_experts(summed[t])
        recon_sum = jnp.einsum("dr,ri->di", returned, place, preferred_element_type=f32)
        recon_full = recon_sum + b_dec[t][:, None]
        recons.append(recon_full.astype(bf16).T)
        error = (
            coef * live_wide[None, :] * (recon_full - targets[t].T.astype(f32))
        ).astype(bf16)
        errors.append(jnp.sum(error.astype(f32), axis=1))
        outgoing = jnp.einsum(
            "di,ri->dr", error, place, preferred_element_type=f32
        ).astype(bf16)
        parts.append(exchange_experts(outgoing))
    recon = jnp.stack(recons)
    grad_b_dec = sum_all(jnp.stack(errors), ("dp", "expert"))
    beside = parts[1:] + [None]
    segments = []
    for t in range(targets_count):
        segment, beside[t] = gather_layers(parts[t], beside[t])
        if t + 1 < targets_count:
            parts[t + 1] = beside[t]
        segments.append(segment)

    grad_lat = sum(
        jnp.einsum("dr,ld->rl", segments[t], w_dec[t, 0], preferred_element_type=f32)
        for t in range(targets_count)
    )
    dec_parts = [
        share_sum(
            lambda rows: jnp.einsum("dr,rl->dl", rows, latents, preferred_element_type=f32),
            segments[t],
            bf16,
        ).astype(bf16)
        for t in range(targets_count)
    ]
    grad_pre = (grad_lat * (2.0 * active)).astype(bf16)
    enc_share = share_sum(
        lambda rows: jnp.einsum("dr,rl->dl", rows, grad_pre, preferred_element_type=f32),
        arrived,
        bf16,
    ).astype(bf16)
    grad_bias = jnp.sum(lax.optimization_barrier(grad_pre).astype(f32), axis=0)
    bias_share = share_sum(lambda rows: rows, grad_bias, f32)
    dec_share = jnp.stack([part.T for part in dec_parts])[:, None]
    return (recon, enc_share[None], bias_share[None], dec_share, grad_b_dec)


MESH = pl.DeviceIdType.MESH
COPIES = 112


def rows_by_rows(left, right):
    return lax.dot_general(
        left, right, (((1,), (1,)), ((), ())), preferred_element_type=jnp.float32
    )


def step_kernel(
    coef,
    cells,
    wanted,
    live,
    place_t,
    b_enc,
    b_dec,
    w_enc,
    w_dec,
    recon_out,
    enc_out,
    bias_out,
    dec_out,
    bdec_out,
    enc_in,
    enc_t,
    dec_in,
    dec_t,
    xin,
    goal,
    alive,
    latents,
    active,
    grad_pre,
    partial,
    first_x,
    first_y,
    next_x,
    next_y,
    last_x,
    last_y,
    errors,
    back_out,
    back_in,
    dec_sent,
    dec_came,
    enc_sent,
    enc_came,
    bias_sent,
    bias_came,
    err_sum,
    err_came,
    err_all,
    send_sem,
    recv_sem,
    load_sem,
):
    f32, bf16 = jnp.float32, jnp.bfloat16
    layer = lax.axis_index("layer")
    expert = lax.axis_index("expert")
    core = lax.axis_index("dp")
    low, high = layer % 2, layer // 2
    along_x = {"layer": high * 2 + 1 - low}
    along_y = {"layer": (1 - high) * 2 + low}
    facing = 3 - layer
    peers = {
        1: {"expert": expert + 1 - 2 * (expert % 2)},
        2: {"expert": (expert + 2) % 4},
        3: {"expert": 3 - expert},
    }
    twin = {"dp": 1 - core}

    width, count = cells.shape
    targets = wanted.shape[0]
    latent = w_enc.shape[1]
    quarter = width // 4
    half = quarter // 2
    share = width // 2
    cap = count // 4
    blocks = 4

    def lanes(block):
        return pl.ds(block * cap, cap)

    def rows(start, size):
        return pl.ds(pl.multiple_of(start, 16), size)

    sends = []

    def send(source, target, device):
        number = len(sends)
        copy = pltpu.make_async_remote_copy(
            src_ref=source,
            dst_ref=target,
            send_sem=send_sem.at[number],
            recv_sem=recv_sem.at[number],
            device_id=device,
            device_id_type=MESH,
        )
        copy.start()
        sends.append(copy)
        return copy

    barrier = pltpu.get_barrier_semaphore()
    partners = [peers[1], peers[2], peers[3], along_x, along_y, twin]
    for partner in partners:
        pl.semaphore_signal(barrier, inc=1, device_id=partner, device_id_type=MESH)
    loads = [
        pltpu.make_async_copy(source, target, load_sem.at[number])
        for number, (source, target) in enumerate(
            [(w_enc, enc_in), (cells.at[:, lanes(0)], xin.at[:, lanes(0)])]
            + [(w_dec.at[t], dec_in.at[t]) for t in range(targets)]
            + [(wanted.at[:, :, lanes(0)], goal.at[:, :, lanes(0)])]
        )
    ]
    for load in loads:
        load.start()
    pl.semaphore_wait(barrier, len(partners))

    own = rows(layer * quarter, quarter)
    other = rows(facing * quarter, quarter)
    near_x = rows((high * 2 + 1 - low) * quarter, quarter)
    near_y = rows(((1 - high) * 2 + low) * quarter, quarter)
    straight = {}
    across = {}
    flags = {}
    goals = {}
    for m in (1, 2, 3):
        straight[m] = send(cells.at[own, lanes(m)], xin.at[own, lanes(m)], peers[m])
    for m in (1, 2, 3):
        across[m] = send(cells.at[other, lanes(m)], xin.at[other, lanes(m)], peers[m])
    for m in (1, 2, 3):
        flags[m] = send(live.at[:, lanes(m)], alive.at[:, lanes(m)], peers[m])
        goals[m] = send(wanted.at[:, :, lanes(m)], goal.at[:, :, lanes(m)], peers[m])

    alive[:, lanes(0)] = live[:, lanes(0)]

    spread = {}

    def forward(k):
        straight[k].wait_recv()
        spread[k] = [
            send(xin.at[own, lanes(k)], xin.at[own, lanes(k)], along_x),
            send(xin.at[own, lanes(k)], xin.at[own, lanes(k)], along_y),
        ]

    def encode(k):
        if k:
            across[k].wait_recv()
            for copy in spread[k]:
                copy.wait_recv()
        tile = 256

        @pl.loop(0, latent // tile)
        def _(i):
            part = rows(i * tile, tile)
            pre = jnp.dot(enc_t[part, :], xin[:, lanes(k)], preferred_element_type=f32)
            value = jnp.maximum(pre + b_enc[part, :], 0.0)
            active[part, lanes(k)] = value
            latents[part, lanes(k)] = (value * value).astype(bf16)

    reduced = {}

    def decode(k, t):
        @pl.loop(0, 4)
        def _(q):
            product = jnp.dot(
                dec_t[t, rows(q * quarter, quarter), :],
                latents[:, lanes(k)],
                preferred_element_type=f32,
            ).astype(bf16)
            partial[k, t, q // 2, q % 2, 0] = product[:half]
            partial[k, t, q // 2, q % 2, 1] = product[half:]

        reduced[k, t] = [
            send(partial.at[k, t, :, 1 - low, 0], first_x.at[k, t], along_x),
            send(partial.at[k, t, 1 - high, :, 1], first_y.at[k, t], along_y),
        ]

    settled = {}

    def combine(k, t):
        for copy in reduced[k, t]:
            copy.wait_recv()
        next_y[k, t] = (
            partial[k, t, 1 - high, low, 0].astype(f32) + first_x[k, t, 1 - high].astype(f32)
        ).astype(bf16)
        next_x[k, t] = (
            partial[k, t, high, 1 - low, 1].astype(f32) + first_y[k, t, 1 - low].astype(f32)
        ).astype(bf16)
        settled[k, t] = [
            send(next_y.at[k, t], last_y.at[k, t], along_y),
            send(next_x.at[k, t], last_x.at[k, t], along_x),
        ]

    gathered = {}
    returned = {}

    def judge(k, t):
        for copy in settled[k, t]:
            copy.wait_recv()
        if k and t == 0:
            flags[k].wait_recv()
            goals[k].wait_recv()
        scale = alive[0:1, lanes(k)] * coef
        for h, (mine, late) in enumerate(
            ((first_x[k, t, high], last_y[k, t]), (first_y[k, t, low], last_x[k, t]))
        ):
            total = partial[k, t, high, low, h].astype(f32) + mine.astype(f32)
            total = (total + late.astype(f32)).astype(bf16).astype(f32)
            part = pl.ds(h * half, half)
            full = total + b_dec[t, part, :]
            if k:
                back_out[k, t, part, :] = full.astype(bf16)
            else:
                back_in[t, part, lanes(0)] = full.astype(bf16)
            gap = full - goal[t, part, lanes(k)].astype(f32)
            errors[t, rows(layer * quarter + h * half, half), lanes(k)] = (
                scale * gap
            ).astype(bf16)
        gathered[k, t] = [
            send(errors.at[t, own, lanes(k)], errors.at[t, own, lanes(k)], along_x),
            send(errors.at[t, own, lanes(k)], errors.at[t, own, lanes(k)], along_y),
        ]
        if k:
            returned[k, t] = send(back_out.at[k, t], back_in.at[t, :, lanes(k)], peers[k])

    relayed = {}

    def relay(k, t):
        for copy in gathered[k, t]:
            copy.wait_recv()
        from_x = errors.at[t, rows((high * 2 + 1 - low) * quarter, half), lanes(k)]
        from_y = errors.at[t, rows(((1 - high) * 2 + low) * quarter + half, half), lanes(k)]
        relayed[k, t] = [send(from_x, from_x, along_y), send(from_y, from_y, along_x)]

    def backward(k):
        for t in range(targets):
            for copy in relayed[k, t]:
                copy.wait_recv()
        tile = 256

        @pl.loop(0, latent // tile)
        def _(i):
            part = rows(i * tile, tile)
            total = sum(
                jnp.dot(dec_in[t, part, :], errors[t, :, lanes(k)], preferred_element_type=f32)
                for t in range(targets)
            )
            grad_pre[part, lanes(k)] = (total * (2.0 * active[part, lanes(k)])).astype(bf16)

    def each(stage, k):
        for t in range(targets):
            stage(k, t)

    step = 256
    loads[0].wait()

    @pl.loop(0, width // step)
    def _(i):
        part = rows(i * step, step)
        enc_t[:, part] = enc_in[part, :].T

    loads[1].wait()
    encode(0)
    for t in range(targets):
        loads[2 + t].wait()

        @pl.loop(0, width // step)
        def _(i):
            part = rows(i * step, step)
            dec_t[t, part, :] = dec_in[t, :, part].T

        decode(0, t)
    loads[2 + targets].wait()
    forward(1)
    each(combine, 0)
    forward(2)
    forward(3)
    for k in range(1, blocks + 1):
        if k < blocks:
            encode(k)
            each(decode, k)
        if k >= 2:
            backward(k - 2)
        each(judge, k - 1)
        if k < blocks:
            each(combine, k)
        each(relay, k - 1)

    ones = jnp.ones((8, count), bf16)
    for t in range(targets):
        err_sum[t] = rows_by_rows(ones, errors[t, own, :])
    err_swap = send(err_sum, err_came, twin)

    third = share // 3

    def dec_product(t, start):
        return rows_by_rows(latents[...], errors[t, rows(start, third), :])

    backward(blocks - 1)
    dec_swap = []
    for t in range(targets):

        @pl.loop(0, 3)
        def _(j):
            dec_sent[t, :, pl.ds(pl.multiple_of(j * third, 128), third)] = dec_product(
                t, (1 - core) * share + j * third
            ).astype(bf16)

        dec_swap.append(send(dec_sent.at[t], dec_came.at[t], twin))

    bias = rows_by_rows(ones, grad_pre[...])
    bias_sent[...] = bias
    side = latent // 2
    mine = pl.ds(pl.multiple_of(core * side, 128), side)
    theirs = pl.ds(pl.multiple_of((1 - core) * side, 128), side)
    bias_swap = send(bias_sent.at[:, theirs], bias_came, twin)

    def enc_product(start):
        return rows_by_rows(xin[rows(start, third), :], grad_pre[...])

    @pl.loop(0, 3)
    def _(j):
        enc_sent[rows(j * third, third), :] = enc_product(
            (1 - core) * share + j * third
        ).astype(bf16)

    enc_swap = send(enc_sent, enc_came, twin)

    err_swap.wait_recv()
    err_all[expert] = err_sum[...] + err_came[...]
    err_spread = [
        send(err_all.at[expert], err_all.at[expert], peers[m]) for m in (1, 2, 3)
    ]

    for t in range(targets):
        dec_swap[t].wait_recv()

        @pl.loop(0, 3)
        def _(j):
            part = pl.ds(pl.multiple_of(j * third, 128), third)
            dec_out[t, :, part] = (
                dec_product(t, core * share + j * third) + dec_came[t, :, part].astype(f32)
            ).astype(bf16)

    enc_swap.wait_recv()

    @pl.loop(0, 3)
    def _(j):
        part = rows(j * third, third)
        enc_out[part, :] = (
            enc_product(core * share + j * third) + enc_came[part, :].astype(f32)
        ).astype(bf16)

    bias_swap.wait_recv()
    bias_out[...] = bias_sent[0:1, mine] + bias_came[0:1, :]

    for k in range(1, blocks):
        for t in range(targets):
            returned[k, t].wait_recv()
    for t in range(targets):
        recon_out[t] = rows_by_rows(place_t[...], back_in[t]).astype(bf16)

    for copy in err_spread:
        copy.wait_recv()
    for t in range(targets):
        total = err_all[0, t] + err_all[1, t] + err_all[2, t] + err_all[3, t]
        bdec_out[t : t + 1, :] = total[0:1]

    for copy in sends:
        copy.wait_send()


def local(tokens, expert_ids, slot_ids, live_mask, w_enc, b_enc, w_dec, b_dec, targets):
    f32, bf16 = jnp.float32, jnp.bfloat16
    n_expert = lax.axis_size("expert")
    n_layer = lax.axis_size("layer")
    assert lax.axis_size("dp") == 2
    if n_expert != 4 or n_layer != 4:
        return plain(
            tokens, expert_ids, slot_ids, live_mask, w_enc, b_enc, w_dec, b_dec, targets
        )
    tok_rows, width = tokens.shape
    cap = 2 * tok_rows // n_expert
    count = n_expert * cap
    quarter, share = width // 4, width // 2
    half = quarter // 2
    latent = w_enc.shape[2]
    kinds = w_dec.shape[0]
    cell_index = (expert_ids ^ lax.axis_index("expert")) * cap + slot_ids
    place = (
        lax.broadcasted_iota(jnp.int32, (count, tok_rows), 0) == cell_index[None, :]
    ).astype(bf16)
    place_t = (
        lax.broadcasted_iota(jnp.int32, (tok_rows, count), 1) == cell_index[:, None]
    ).astype(bf16)
    cells = lax.dot_general(
        tokens, place, (((0,), (1,)), ((), ())), preferred_element_type=f32
    ).astype(bf16)
    wanted = jnp.einsum("tid,ri->tdr", targets, place, preferred_element_type=f32).astype(bf16)
    live = jnp.einsum(
        "i,ri->r", live_mask.astype(bf16), place, preferred_element_type=f32
    )
    live = jnp.broadcast_to(live[None], (8, count))
    b_enc_wide = jnp.broadcast_to(b_enc[0][:, None], (latent, cap))
    b_dec_wide = jnp.broadcast_to(b_dec[:, :, None], (kinds, quarter, cap))
    coef = 2.0 / math.sqrt(tok_rows)

    vmem = pl.BlockSpec(memory_space=pltpu.VMEM)
    hbm = pl.BlockSpec(memory_space=pl.ANY)
    scratch = [
        ((width, latent), bf16),
        ((latent, width), bf16),
        ((kinds, latent, width), bf16),
        ((kinds, width, latent), bf16),
        ((width, count), bf16),
        ((kinds, quarter, count), bf16),
        ((8, count), f32),
        ((latent, count), bf16),
        ((latent, count), f32),
        ((latent, count), bf16),
        ((4, kinds, 2, 2, 2, half, cap), bf16),
        ((4, kinds, 2, half, cap), bf16),
        ((4, kinds, 2, half, cap), bf16),
        ((4, kinds, half, cap), bf16),
        ((4, kinds, half, cap), bf16),
        ((4, kinds, half, cap), bf16),
        ((4, kinds, half, cap), bf16),
        ((kinds, width, count), bf16),
        ((4, kinds, quarter, cap), bf16),
        ((kinds, quarter, count), bf16),
        ((kinds, latent, share), bf16),
        ((kinds, latent, share), bf16),
        ((share, latent), bf16),
        ((share, latent), bf16),
        ((8, latent), f32),
        ((8, latent // 2), f32),
        ((kinds, 8, quarter), f32),
        ((kinds, 8, quarter), f32),
        ((4, kinds, 8, quarter), f32),
    ]
    recon, enc, bias, dec, bdec = pl.pallas_call(
        functools.partial(step_kernel, coef),
        out_shape=(
            jax.ShapeDtypeStruct((kinds, tok_rows, quarter), bf16),
            jax.ShapeDtypeStruct((share, latent), bf16),
            jax.ShapeDtypeStruct((1, latent // 2), f32),
            jax.ShapeDtypeStruct((kinds, latent, share), bf16),
            jax.ShapeDtypeStruct((kinds, quarter), f32),
        ),
        in_specs=[hbm, hbm, vmem, vmem, vmem, vmem, hbm, hbm],
        out_specs=(vmem,) * 5,
        scratch_shapes=[pltpu.VMEM(shape, dtype) for shape, dtype in scratch]
        + [
            pltpu.SemaphoreType.DMA((COPIES,)),
            pltpu.SemaphoreType.DMA((COPIES,)),
            pltpu.SemaphoreType.DMA((3 + kinds,)),
        ],
        compiler_params=pltpu.CompilerParams(
            collective_id=0, has_side_effects=True, vmem_limit_bytes=62 * 2**20
        ),
        name="step",
    )(cells, wanted, live, place_t, b_enc_wide, b_dec_wide, w_enc[0], w_dec[:, 0])
    return (recon, enc[None], bias, dec[:, None], bdec)


def solution(mesh):
    placed = (
        P(("expert", "dp"), None),
        P(("expert", "dp")),
        P(("expert", "dp")),
        P(("expert", "dp")),
        P("expert", None, "layer"),
        P("expert", "layer"),
        P(None, "expert", "layer", None),
        P(None, "layer"),
        P(None, ("expert", "dp"), "layer"),
    )
    return jax.shard_map(
        local,
        mesh=mesh,
        in_specs=placed,
        out_specs=(
            P(None, ("expert", "dp"), "layer"),
            P("expert", "dp", "layer"),
            P("expert", ("layer", "dp")),
            P(None, "expert", "layer", "dp"),
            P(None, "layer"),
        ),
        check_vma=False,
    )
```

```python
import math

import jax
import jax.numpy as jnp
from jax import lax
from jax.experimental import pallas as pl
from jax.experimental.pallas import tpu as pltpu
from jax.sharding import PartitionSpec as P


def swap(values, mask, axis="layer"):
    size = lax.axis_size(axis)
    return lax.ppermute(values, axis, [(i, i ^ mask) for i in range(size)])


def exchange_experts(values):
    size = lax.axis_size("expert")
    if size != 4:
        return lax.all_to_all(values, "expert", split_axis=1, concat_axis=1, tiled=True)
    width = values.shape[1] // size
    blocks = [values[:, k * width : (k + 1) * width] for k in range(size)]
    for mask in (2, 3, 1):
        blocks[mask] = swap(blocks[mask], mask, "expert")
    return jnp.concatenate(blocks, axis=1)


def sum_all(values, axes):
    for axis in axes:
        size = lax.axis_size(axis)
        if size & (size - 1):
            values = lax.psum(values, axis)
            continue
        mask = 1
        while mask < size:
            values = values + swap(values, mask, axis)
            mask *= 2
    return values


def share_sum(product, rows, fills):
    depth = rows.shape[0] // 2
    me = lax.axis_index("dp")
    sent = product(lax.dynamic_slice_in_dim(rows, (1 - me) * depth, depth, 0))
    came = swap(sent.astype(fills), 1, "dp")
    own = product(lax.dynamic_slice_in_dim(rows, me * depth, depth, 0))
    return own + came.astype(jnp.float32)


def gather_layers(piece, beside=None):
    size = lax.axis_size("layer")
    if size != 4 or piece.shape[0] % 2:
        return lax.all_gather(piece, "layer", axis=0, tiled=True), beside
    me = lax.axis_index("layer")
    depth = piece.shape[0]
    half = depth // 2
    near = swap(piece, 1)
    far = swap(piece, 2)
    if beside is not None:
        near, far, beside = lax.optimization_barrier((near, far, beside))
    first = swap(far[:half], 1)
    second = swap(near[half:], 2)
    whole = jnp.zeros((size * depth,) + piece.shape[1:], piece.dtype)
    for offset, value in (
        (me * depth, piece),
        ((me ^ 1) * depth, near),
        ((me ^ 2) * depth, far),
        ((me ^ 3) * depth, first),
        ((me ^ 3) * depth + half, second),
    ):
        whole = lax.dynamic_update_slice_in_dim(whole, value, offset, 0)
    return whole, beside


def scatter_sum(values):
    size = lax.axis_size("layer")
    depth = values.shape[0] // size
    if size != 4 or depth % 2:
        return lax.psum_scatter(values, "layer", scatter_dimension=0, tiled=True)
    f32 = jnp.float32
    me = lax.axis_index("layer")
    low, high = me % 2, me // 2
    pieces = values.reshape((2, 2, 2, depth // 2) + values.shape[1:])

    def pick(array, index, axis):
        return lax.dynamic_index_in_dim(array, index, axis, keepdims=False)

    one, two = pieces[:, :, 0], pieces[:, :, 1]
    one_in = swap(pick(one, 1 - low, 1), 1)
    two_in = swap(pick(two, 1 - high, 0), 2)
    one_sum = pick(one, low, 1).astype(f32) + one_in.astype(f32)
    two_sum = pick(two, high, 0).astype(f32) + two_in.astype(f32)
    one_last = swap(pick(one_sum, 1 - high, 0).astype(values.dtype), 2)
    two_last = swap(pick(two_sum, 1 - low, 0).astype(values.dtype), 1)
    return jnp.concatenate(
        [
            (pick(one_sum, high, 0) + one_last.astype(f32)).astype(values.dtype),
            (pick(two_sum, low, 0) + two_last.astype(f32)).astype(values.dtype),
        ]
    )


def plain(tokens, expert_ids, slot_ids, live_mask, w_enc, b_enc, w_dec, b_dec, targets):
    f32, bf16 = jnp.float32, jnp.bfloat16
    n_expert = lax.axis_size("expert")
    n_layer = lax.axis_size("layer")
    assert lax.axis_size("dp") == 2
    tok_rows, model_width = tokens.shape
    capacity = 2 * tok_rows // n_expert
    total_cells = n_expert * capacity
    offset = lax.axis_index("expert") if n_expert == 4 else 0
    cell_index = (expert_ids ^ offset) * capacity + slot_ids
    quarter = model_width // n_layer
    targets_count = w_dec.shape[0]
    enc_weight = w_enc[0]
    place = (
        lax.broadcasted_iota(jnp.int32, (total_cells, tok_rows), 0) == cell_index[None, :]
    ).astype(bf16)

    cells = lax.dot_general(
        tokens, place, (((0,), (1,)), ((), ())), preferred_element_type=f32
    ).astype(bf16)
    own = lax.dynamic_slice_in_dim(cells, lax.axis_index("layer") * quarter, quarter, 0)
    arrived_part = exchange_experts(own)
    arrived, _ = gather_layers(arrived_part)
    pre_act = jnp.einsum("dr,dl->rl", arrived, enc_weight, preferred_element_type=f32)
    pre_act = pre_act + b_enc[0][None, :]
    active = jnp.maximum(pre_act, 0.0)
    latents = (active * active).astype(bf16)

    coef = 2.0 / math.sqrt(tok_rows)
    live_wide = live_mask.astype(f32)
    partials = [
        jnp.einsum("ld,rl->dr", w_dec[t, 0], latents, preferred_element_type=f32).astype(bf16)
        for t in range(targets_count)
    ]
    summed = [scatter_sum(p) for p in partials]
    recons, errors, parts = [], [], []
    for t in range(targets_count):
        returned = exchange_experts(summed[t])
        recon_sum = jnp.einsum("dr,ri->di", returned, place, preferred_element_type=f32)
        recon_full = recon_sum + b_dec[t][:, None]
        recons.append(recon_full.astype(bf16).T)
        error = (
            coef * live_wide[None, :] * (recon_full - targets[t].T.astype(f32))
        ).astype(bf16)
        errors.append(jnp.sum(error.astype(f32), axis=1))
        outgoing = jnp.einsum(
            "di,ri->dr", error, place, preferred_element_type=f32
        ).astype(bf16)
        parts.append(exchange_experts(outgoing))
    recon = jnp.stack(recons)
    grad_b_dec = sum_all(jnp.stack(errors), ("dp", "expert"))
    beside = parts[1:] + [None]
    segments = []
    for t in range(targets_count):
        segment, beside[t] = gather_layers(parts[t], beside[t])
        if t + 1 < targets_count:
            parts[t + 1] = beside[t]
        segments.append(segment)

    grad_lat = sum(
        jnp.einsum("dr,ld->rl", segments[t], w_dec[t, 0], preferred_element_type=f32)
        for t in range(targets_count)
    )
    dec_parts = [
        share_sum(
            lambda rows: jnp.einsum("dr,rl->dl", rows, latents, preferred_element_type=f32),
            segments[t],
            bf16,
        ).astype(bf16)
        for t in range(targets_count)
    ]
    grad_pre = (grad_lat * (2.0 * active)).astype(bf16)
    enc_share = share_sum(
        lambda rows: jnp.einsum("dr,rl->dl", rows, grad_pre, preferred_element_type=f32),
        arrived,
        bf16,
    ).astype(bf16)
    grad_bias = jnp.sum(lax.optimization_barrier(grad_pre).astype(f32), axis=0)
    bias_share = share_sum(lambda rows: rows, grad_bias, f32)
    dec_share = jnp.stack([part.T for part in dec_parts])[:, None]
    return (recon, enc_share[None], bias_share[None], dec_share, grad_b_dec)


MESH = pl.DeviceIdType.MESH
COPIES = 128


def rows_by_rows(left, right):
    return lax.dot_general(
        left, right, (((1,), (1,)), ((), ())), preferred_element_type=jnp.float32
    )


def step_kernel(
    expert_ids,
    slot_ids,
    live_mask,
    b_enc,
    b_dec,
    tokens,
    targets,
    w_enc,
    w_dec,
    recon_out,
    enc_out,
    bias_out,
    dec_out,
    bdec_out,
    tok_in,
    tok_t,
    goal_in,
    place,
    bias_pad,
    enc_wide,
    dec_wide,
    cells_out,
    goal_out,
    alive_out,
    enc_in,
    enc_t,
    dec_in,
    dec_t,
    xin,
    goal,
    alive,
    latents,
    active,
    grad_lat,
    grad_pre,
    partial,
    first_x,
    first_y,
    next_x,
    next_y,
    last_x,
    last_y,
    errors,
    back_out,
    back_in,
    dec_sum,
    enc_sum,
    err_sum,
    err_came,
    err_all,
    send_sem,
    recv_sem,
    load_sem,
):
    f32, bf16 = jnp.float32, jnp.bfloat16
    layer = lax.axis_index("layer")
    expert = lax.axis_index("expert")
    core = lax.axis_index("dp")
    low, high = layer % 2, layer // 2
    beside_x = high * 2 + 1 - low
    beside_y = (1 - high) * 2 + low
    facing = 3 - layer
    along_x, along_y = {"layer": beside_x}, {"layer": beside_y}
    peers = {
        1: {"expert": expert + 1 - 2 * (expert % 2)},
        2: {"expert": (expert + 2) % 4},
        3: {"expert": 3 - expert},
    }
    twin = {"dp": 1 - core}

    tok_rows, width = tok_in.shape
    kinds = goal_in.shape[0]
    latent = enc_in.shape[1]
    count = place.shape[0]
    quarter = width // 4
    half = quarter // 2
    share = width // 2
    cap = count // 4
    coef = 2.0 / math.sqrt(tok_rows)

    def lanes(block):
        return pl.ds(block * 2 * cap, cap)

    def twin_lanes(block):
        return pl.ds(block * 2 * cap + cap, cap)

    def pair(block):
        return pl.ds(block * 2 * cap, 2 * cap)

    def slots(block):
        return pl.ds(block * cap, cap)

    def rows(start, size):
        return pl.ds(pl.multiple_of(start, 16), size)

    sends = []

    def send(source, target, device):
        number = len(sends)
        copy = pltpu.make_async_remote_copy(
            src_ref=source,
            dst_ref=target,
            send_sem=send_sem.at[number],
            recv_sem=recv_sem.at[number],
            device_id=device,
            device_id_type=MESH,
        )
        copy.start()
        sends.append(copy)
        return copy

    barrier = pltpu.get_barrier_semaphore()
    partners = [peers[1], peers[2], peers[3], along_x, along_y, twin]
    for partner in partners:
        pl.semaphore_signal(barrier, inc=1, device_id=partner, device_id_type=MESH)
    load_tokens, load_enc, load_dec, load_goal = loads = [
        pltpu.make_async_copy(source, target, load_sem.at[number])
        for number, (source, target) in enumerate(
            [(tokens, tok_in), (w_enc, enc_in), (w_dec, dec_in), (targets, goal_in)]
        )
    ]
    for load in loads:
        load.start()

    own = rows(layer * quarter, quarter)
    other = rows(facing * quarter, quarter)
    step = 256

    cell = (expert_ids[...] ^ expert) * cap + slot_ids[...]
    marks = lax.broadcasted_iota(jnp.int32, (count, tok_rows), 0) == cell
    place[...] = jnp.where(marks, 1.0, 0.0).astype(bf16)
    load_tokens.wait()

    @pl.loop(0, width // step)
    def _(i):
        part = rows(i * step, step)
        tok_t[part, :] = tok_in[:, part].T

    def pack(number, part):
        cells_out[number] = rows_by_rows(tok_t[part, :], place[cap:, :]).astype(bf16)

    straight, across, flags, goals = {}, {}, {}, {}
    pack(0, own)
    pl.semaphore_wait(barrier, len(partners))
    for m in (1, 2, 3):
        straight[m] = send(
            cells_out.at[0, :, slots(m - 1)], xin.at[own, lanes(m)], peers[m]
        )
    pack(1, other)
    for m in (1, 2, 3):
        across[m] = send(
            cells_out.at[1, :, slots(m - 1)], xin.at[other, lanes(m)], peers[m]
        )

    @pl.loop(0, 4)
    def _(q):
        part = rows(q * quarter, quarter)
        xin[part, lanes(0)] = rows_by_rows(tok_t[part, :], place[:cap, :]).astype(bf16)

    bias_pad[:, :latent] = jnp.broadcast_to(b_enc[...], (cap, latent))
    enc_wide[...] = bias_pad[:, :latent].T
    load_enc.wait()

    @pl.loop(0, width // step)
    def _(i):
        part = rows(i * step, step)
        enc_t[:, part] = enc_in[part, :].T

    def share_rows(ref, k, part):
        return send(ref.at[part, lanes(k)], ref.at[part, twin_lanes(k)], twin)

    theirs = rows((1 - core) * share, share)
    spread, traded = {}, {}

    def forward(k):
        straight[k].wait_recv()
        spread[k] = [
            send(xin.at[own, lanes(k)], xin.at[own, lanes(k)], along_x),
            send(xin.at[own, lanes(k)], xin.at[own, lanes(k)], along_y),
        ]

    def encode(k):
        if k:
            across[k].wait_recv()
            for copy in spread[k]:
                copy.wait_recv()

        @pl.loop(0, latent // step)
        def _(i):
            part = rows(i * step, step)
            pre = jnp.dot(enc_t[part, :], xin[:, lanes(k)], preferred_element_type=f32)
            value = jnp.maximum(pre + enc_wide[part, :], 0.0)
            active[part, slots(k)] = value
            latents[part, lanes(k)] = (value * value).astype(bf16)

    def trade(k):
        everything = rows(0, latent)
        traded[k] = [share_rows(latents, k, everything), share_rows(xin, k, theirs)]

    reduced = {}

    def decode(k, t):
        @pl.loop(0, 4)
        def _(q):
            product = jnp.dot(
                dec_t[t, rows(q * quarter, quarter), :],
                latents[:, lanes(k)],
                preferred_element_type=f32,
            ).astype(bf16)
            partial[k, t, q // 2, q % 2, 0] = product[:half]
            partial[k, t, q // 2, q % 2, 1] = product[half:]

        reduced[k, t] = [
            send(partial.at[k, t, :, 1 - low, 0], first_x.at[k, t], along_x),
            send(partial.at[k, t, 1 - high, :, 1], first_y.at[k, t], along_y),
        ]

    settled = {}

    def combine(k, t):
        for copy in reduced[k, t]:
            copy.wait_recv()
        next_y[k, t] = (
            partial[k, t, 1 - high, low, 0].astype(f32) + first_x[k, t, 1 - high].astype(f32)
        ).astype(bf16)
        next_x[k, t] = (
            partial[k, t, high, 1 - low, 1].astype(f32) + first_y[k, t, 1 - low].astype(f32)
        ).astype(bf16)
        settled[k, t] = [
            send(next_y.at[k, t], last_y.at[k, t], along_y),
            send(next_x.at[k, t], last_x.at[k, t], along_x),
        ]

    gathered, returned = {}, {}

    def judge(k, t):
        for copy in settled[k, t]:
            copy.wait_recv()
        if k and t == 0:
            flags[k].wait_recv()
            goals[k].wait_recv()
        scale = alive[0:1, slots(k)] * coef
        for h, (mine, late) in enumerate(
            ((first_x[k, t, high], last_y[k, t]), (first_y[k, t, low], last_x[k, t]))
        ):
            total = partial[k, t, high, low, h].astype(f32) + mine.astype(f32)
            total = (total + late.astype(f32)).astype(bf16).astype(f32)
            part = pl.ds(h * half, half)
            full = total + dec_wide[t, part, :]
            if k:
                back_out[k - 1, t, part, :] = full.astype(bf16)
            else:
                back_in[t, part, slots(0)] = full.astype(bf16)
            gap = full - goal[t, part, slots(k)].astype(f32)
            errors[t, rows(layer * quarter + h * half, half), lanes(k)] = (
                scale * gap
            ).astype(bf16)
        piece = errors.at[t, own, lanes(k)]
        gathered[k, t] = [send(piece, piece, along_x), send(piece, piece, along_y)]

    def give_back(k, t):
        returned[k, t] = send(back_out.at[k - 1, t], back_in.at[t, :, slots(k)], peers[k])

    relayed = {}

    def relay(k, t):
        for copy in gathered[k, t]:
            copy.wait_recv()
        from_x = errors.at[t, rows(beside_x * quarter, half), lanes(k)]
        from_y = errors.at[t, rows(beside_y * quarter + half, half), lanes(k)]
        relayed[k, t] = [send(from_x, from_x, along_y), send(from_y, from_y, along_x)]

    handed = {}

    def backward(k, t):
        for copy in relayed[k, t]:
            copy.wait_recv()
        handed[k, t] = share_rows(errors.at[t], k, theirs)

        @pl.loop(0, latent // step)
        def _(i):
            part = rows(i * step, step)
            value = jnp.dot(dec_in[t, part, :], errors[t, :, lanes(k)], preferred_element_type=f32)
            if t:
                value = value + grad_lat[part, :]
            if t < kinds - 1:
                grad_lat[part, :] = value
            else:
                grad_pre[part, lanes(k)] = (
                    value * (2.0 * active[part, slots(k)])
                ).astype(bf16)

        if t == kinds - 1:
            handed[k] = share_rows(grad_pre, k, rows(0, latent))

    third = share // 3
    final = 3

    def grow_dec(k, t):
        if t == 0:
            for copy in traded[k]:
                copy.wait_recv()
        handed[k, t].wait_recv()

        @pl.loop(0, 3)
        def _(j):
            part = pl.ds(pl.multiple_of(j * third, 128), third)
            value = rows_by_rows(
                latents[:, pair(k)], errors[t, rows(core * share + j * third, third), pair(k)]
            )
            if k:
                value = value + dec_sum[t, :, part]
            if k < final:
                dec_sum[t, :, part] = value
            else:
                dec_out[t, :, part] = value.astype(bf16)

    def grow_enc(k):
        handed[k].wait_recv()

        @pl.loop(0, 3)
        def _(j):
            part = rows(j * third, third)
            value = rows_by_rows(
                xin[rows(core * share + j * third, third), pair(k)], grad_pre[:, pair(k)]
            )
            if k:
                value = value + enc_sum[part, :]
            if k < final:
                enc_sum[part, :] = value
            else:
                enc_out[part, :] = value.astype(bf16)

    def each(stage, *key):
        for t in range(kinds):
            stage(*key, t)

    encode(0)
    load_dec.wait()
    for t in range(kinds):

        @pl.loop(0, width // step)
        def _(i):
            part = rows(i * step, step)
            dec_t[t, part, :] = dec_in[t, :, part].T

        decode(0, t)
    trade(0)

    load_goal.wait()
    live = jnp.broadcast_to(live_mask[...].astype(f32).astype(bf16), (8, tok_rows))
    shown = rows_by_rows(live, place[...])
    alive[:, slots(0)] = shown[:, :cap]
    alive_out[...] = shown[:, cap:]
    for t in range(kinds):
        moved = rows_by_rows(goal_in[t], place[...]).astype(bf16)
        goal[t, :, slots(0)] = moved[:, :cap]
        goal_out[t] = moved[:, cap:]
        bias_pad[:, :quarter] = jnp.broadcast_to(b_dec[t : t + 1, :], (cap, quarter))
        dec_wide[t] = bias_pad[...].T[:quarter]
    for m in (1, 2, 3):
        flags[m] = send(alive_out.at[:, slots(m - 1)], alive.at[:, slots(m)], peers[m])
        goals[m] = send(goal_out.at[:, :, slots(m - 1)], goal.at[:, :, slots(m)], peers[m])

    forward(1)
    each(combine, 0)
    forward(2)
    each(judge, 0)
    encode(1)
    each(decode, 1)
    trade(1)
    forward(3)
    each(relay, 0)
    each(combine, 1)
    encode(2)
    each(decode, 2)
    trade(2)
    each(judge, 1)
    each(give_back, 1)
    each(backward, 0)
    each(combine, 2)
    each(relay, 1)
    encode(3)
    each(decode, 3)
    trade(3)
    each(judge, 2)
    each(give_back, 2)
    each(grow_dec, 0)
    grow_enc(0)
    each(backward, 1)
    each(combine, 3)
    each(relay, 2)
    each(grow_dec, 1)
    grow_enc(1)
    judge(3, 0)
    give_back(3, 0)
    judge(3, 1)
    ones = jnp.ones((8, cap), bf16)
    for t in range(kinds):
        err_sum[t] = sum(rows_by_rows(ones, errors[t, own, lanes(k)]) for k in range(4))
    err_swap = send(err_sum, err_came, twin)
    each(backward, 2)
    relay(3, 0)
    err_swap.wait_recv()
    err_all[expert] = err_sum[...] + err_came[...]
    err_spread = [send(err_all.at[expert], err_all.at[expert], peers[m]) for m in (1, 2, 3)]
    give_back(3, 1)
    relay(3, 1)
    each(grow_dec, 2)
    grow_enc(2)
    each(backward, 3)
    each(grow_dec, 3)
    grow_enc(3)

    side = latent // 2
    bias_out[...] = rows_by_rows(
        jnp.ones((8, 8 * cap), bf16), grad_pre[rows(core * side, side), :]
    )[0:1]
    for k in (1, 2, 3):
        for t in range(kinds):
            returned[k, t].wait_recv()
    for t in range(kinds):
        recon_out[t] = jnp.dot(
            back_in[t], place[...], preferred_element_type=f32
        ).astype(bf16)
    for copy in err_spread:
        copy.wait_recv()
    for t in range(kinds):
        total = err_all[0, t] + err_all[1, t] + err_all[2, t] + err_all[3, t]
        bdec_out[t : t + 1, :] = total[0:1]

    for copy in sends:
        copy.wait_send()


def local(tokens, expert_ids, slot_ids, live_mask, w_enc, b_enc, w_dec, b_dec, targets):
    f32, bf16 = jnp.float32, jnp.bfloat16
    n_expert = lax.axis_size("expert")
    n_layer = lax.axis_size("layer")
    assert lax.axis_size("dp") == 2
    if n_expert != 4 or n_layer != 4:
        return plain(
            tokens, expert_ids, slot_ids, live_mask, w_enc, b_enc, w_dec, b_dec, targets
        )
    tok_rows, width = tokens.shape
    cap = 2 * tok_rows // n_expert
    count = n_expert * cap
    quarter, share = width // 4, width // 2
    half = quarter // 2
    padded = -(-quarter // 128) * 128
    latent = w_enc.shape[2]
    kinds = w_dec.shape[0]
    rest = count - cap

    vmem = pl.BlockSpec(memory_space=pltpu.VMEM)
    hbm = pl.BlockSpec(memory_space=pl.ANY)
    scratch = [
        ((tok_rows, width), bf16),
        ((width, tok_rows), bf16),
        ((kinds, quarter, tok_rows), bf16),
        ((count, tok_rows), bf16),
        ((cap, max(padded, latent)), f32),
        ((latent, cap), f32),
        ((kinds, quarter, cap), f32),
        ((2, quarter, rest), bf16),
        ((kinds, quarter, rest), bf16),
        ((8, rest), f32),
        ((width, latent), bf16),
        ((latent, width), bf16),
        ((kinds, latent, width), bf16),
        ((kinds, width, latent), bf16),
        ((width, 2 * count), bf16),
        ((kinds, quarter, count), bf16),
        ((8, count), f32),
        ((latent, 2 * count), bf16),
        ((latent, count), f32),
        ((latent, cap), f32),
        ((latent, 2 * count), bf16),
        ((4, kinds, 2, 2, 2, half, cap), bf16),
        ((4, kinds, 2, half, cap), bf16),
        ((4, kinds, 2, half, cap), bf16),
        ((4, kinds, half, cap), bf16),
        ((4, kinds, half, cap), bf16),
        ((4, kinds, half, cap), bf16),
        ((4, kinds, half, cap), bf16),
        ((kinds, width, 2 * count), bf16),
        ((3, kinds, quarter, cap), bf16),
        ((kinds, quarter, count), bf16),
        ((kinds, latent, share), f32),
        ((share, latent), f32),
        ((kinds, 8, quarter), f32),
        ((kinds, 8, quarter), f32),
        ((4, kinds, 8, quarter), f32),
    ]
    results = [
        ((kinds, quarter, tok_rows), bf16),
        ((share, latent), bf16),
        ((1, latent // 2), f32),
        ((kinds, latent, share), bf16),
        ((kinds, quarter), f32),
    ]
    recon, enc, bias, dec, bdec = pl.pallas_call(
        step_kernel,
        out_shape=tuple(pltpu.VMEM(shape, dtype) for shape, dtype in results),
        in_specs=[vmem] * 5 + [hbm] * 4,
        out_specs=(vmem,) * 5,
        scratch_shapes=[pltpu.VMEM(shape, dtype) for shape, dtype in scratch]
        + [
            pltpu.SemaphoreType.DMA((COPIES,)),
            pltpu.SemaphoreType.DMA((COPIES,)),
            pltpu.SemaphoreType.DMA((4,)),
        ],
        compiler_params=pltpu.CompilerParams(
            collective_id=0, has_side_effects=True, vmem_limit_bytes=60 * 10**6
        ),
        name="step",
    )(
        expert_ids[None],
        slot_ids[None],
        live_mask[None],
        b_enc,
        b_dec,
        tokens,
        jnp.swapaxes(targets, 1, 2),
        w_enc[0],
        w_dec[:, 0],
    )
    return (jnp.swapaxes(recon, 1, 2), enc[None], bias, dec[:, None], bdec)


def solution(mesh):
    placed = (
        P(("expert", "dp"), None),
        P(("expert", "dp")),
        P(("expert", "dp")),
        P(("expert", "dp")),
        P("expert", None, "layer"),
        P("expert", "layer"),
        P(None, "expert", "layer", None),
        P(None, "layer"),
        P(None, ("expert", "dp"), "layer"),
    )
    return jax.shard_map(
        local,
        mesh=mesh,
        in_specs=placed,
        out_specs=(
            P(None, ("expert", "dp"), "layer"),
            P("expert", "dp", "layer"),
            P("expert", ("layer", "dp")),
            P(None, "expert", "layer", "dp"),
            P(None, "layer"),
        ),
        check_vma=False,
    )
```

```python
import math

import jax
import jax.numpy as jnp
from jax import lax
from jax.experimental import pallas as pl
from jax.experimental.pallas import tpu as pltpu
from jax.sharding import PartitionSpec as P


def swap(values, mask, axis="layer"):
    size = lax.axis_size(axis)
    return lax.ppermute(values, axis, [(i, i ^ mask) for i in range(size)])


def exchange_experts(values):
    size = lax.axis_size("expert")
    if size != 4:
        return lax.all_to_all(values, "expert", split_axis=1, concat_axis=1, tiled=True)
    width = values.shape[1] // size
    blocks = [values[:, k * width : (k + 1) * width] for k in range(size)]
    for mask in (2, 3, 1):
        blocks[mask] = swap(blocks[mask], mask, "expert")
    return jnp.concatenate(blocks, axis=1)


def sum_all(values, axes):
    for axis in axes:
        size = lax.axis_size(axis)
        if size & (size - 1):
            values = lax.psum(values, axis)
            continue
        mask = 1
        while mask < size:
            values = values + swap(values, mask, axis)
            mask *= 2
    return values


def share_sum(product, rows, fills):
    depth = rows.shape[0] // 2
    me = lax.axis_index("dp")
    sent = product(lax.dynamic_slice_in_dim(rows, (1 - me) * depth, depth, 0))
    came = swap(sent.astype(fills), 1, "dp")
    own = product(lax.dynamic_slice_in_dim(rows, me * depth, depth, 0))
    return own + came.astype(jnp.float32)


def gather_layers(piece, beside=None):
    size = lax.axis_size("layer")
    if size != 4 or piece.shape[0] % 2:
        return lax.all_gather(piece, "layer", axis=0, tiled=True), beside
    me = lax.axis_index("layer")
    depth = piece.shape[0]
    half = depth // 2
    near = swap(piece, 1)
    far = swap(piece, 2)
    if beside is not None:
        near, far, beside = lax.optimization_barrier((near, far, beside))
    first = swap(far[:half], 1)
    second = swap(near[half:], 2)
    whole = jnp.zeros((size * depth,) + piece.shape[1:], piece.dtype)
    for offset, value in (
        (me * depth, piece),
        ((me ^ 1) * depth, near),
        ((me ^ 2) * depth, far),
        ((me ^ 3) * depth, first),
        ((me ^ 3) * depth + half, second),
    ):
        whole = lax.dynamic_update_slice_in_dim(whole, value, offset, 0)
    return whole, beside


def scatter_sum(values):
    size = lax.axis_size("layer")
    depth = values.shape[0] // size
    if size != 4 or depth % 2:
        return lax.psum_scatter(values, "layer", scatter_dimension=0, tiled=True)
    f32 = jnp.float32
    me = lax.axis_index("layer")
    low, high = me % 2, me // 2
    pieces = values.reshape((2, 2, 2, depth // 2) + values.shape[1:])

    def pick(array, index, axis):
        return lax.dynamic_index_in_dim(array, index, axis, keepdims=False)

    one, two = pieces[:, :, 0], pieces[:, :, 1]
    one_in = swap(pick(one, 1 - low, 1), 1)
    two_in = swap(pick(two, 1 - high, 0), 2)
    one_sum = pick(one, low, 1).astype(f32) + one_in.astype(f32)
    two_sum = pick(two, high, 0).astype(f32) + two_in.astype(f32)
    one_last = swap(pick(one_sum, 1 - high, 0).astype(values.dtype), 2)
    two_last = swap(pick(two_sum, 1 - low, 0).astype(values.dtype), 1)
    return jnp.concatenate(
        [
            (pick(one_sum, high, 0) + one_last.astype(f32)).astype(values.dtype),
            (pick(two_sum, low, 0) + two_last.astype(f32)).astype(values.dtype),
        ]
    )


def plain(tokens, expert_ids, slot_ids, live_mask, w_enc, b_enc, w_dec, b_dec, targets):
    f32, bf16 = jnp.float32, jnp.bfloat16
    n_expert = lax.axis_size("expert")
    n_layer = lax.axis_size("layer")
    assert lax.axis_size("dp") == 2
    tok_rows, model_width = tokens.shape
    capacity = 2 * tok_rows // n_expert
    total_cells = n_expert * capacity
    offset = lax.axis_index("expert") if n_expert == 4 else 0
    cell_index = (expert_ids ^ offset) * capacity + slot_ids
    quarter = model_width // n_layer
    targets_count = w_dec.shape[0]
    enc_weight = w_enc[0]
    place = (
        lax.broadcasted_iota(jnp.int32, (total_cells, tok_rows), 0) == cell_index[None, :]
    ).astype(bf16)

    cells = lax.dot_general(
        tokens, place, (((0,), (1,)), ((), ())), preferred_element_type=f32
    ).astype(bf16)
    own = lax.dynamic_slice_in_dim(cells, lax.axis_index("layer") * quarter, quarter, 0)
    arrived_part = exchange_experts(own)
    arrived, _ = gather_layers(arrived_part)
    pre_act = jnp.einsum("dr,dl->rl", arrived, enc_weight, preferred_element_type=f32)
    pre_act = pre_act + b_enc[0][None, :]
    active = jnp.maximum(pre_act, 0.0)
    latents = (active * active).astype(bf16)

    coef = 2.0 / math.sqrt(tok_rows)
    live_wide = live_mask.astype(f32)
    partials = [
        jnp.einsum("ld,rl->dr", w_dec[t, 0], latents, preferred_element_type=f32).astype(bf16)
        for t in range(targets_count)
    ]
    summed = [scatter_sum(p) for p in partials]
    recons, errors, parts = [], [], []
    for t in range(targets_count):
        returned = exchange_experts(summed[t])
        recon_sum = jnp.einsum("dr,ri->di", returned, place, preferred_element_type=f32)
        recon_full = recon_sum + b_dec[t][:, None]
        recons.append(recon_full.astype(bf16).T)
        error = (
            coef * live_wide[None, :] * (recon_full - targets[t].T.astype(f32))
        ).astype(bf16)
        errors.append(jnp.sum(error.astype(f32), axis=1))
        outgoing = jnp.einsum(
            "di,ri->dr", error, place, preferred_element_type=f32
        ).astype(bf16)
        parts.append(exchange_experts(outgoing))
    recon = jnp.stack(recons)
    grad_b_dec = sum_all(jnp.stack(errors), ("dp", "expert"))
    beside = parts[1:] + [None]
    segments = []
    for t in range(targets_count):
        segment, beside[t] = gather_layers(parts[t], beside[t])
        if t + 1 < targets_count:
            parts[t + 1] = beside[t]
        segments.append(segment)

    grad_lat = sum(
        jnp.einsum("dr,ld->rl", segments[t], w_dec[t, 0], preferred_element_type=f32)
        for t in range(targets_count)
    )
    dec_parts = [
        share_sum(
            lambda rows: jnp.einsum("dr,rl->dl", rows, latents, preferred_element_type=f32),
            segments[t],
            bf16,
        ).astype(bf16)
        for t in range(targets_count)
    ]
    grad_pre = (grad_lat * (2.0 * active)).astype(bf16)
    enc_share = share_sum(
        lambda rows: jnp.einsum("dr,rl->dl", rows, grad_pre, preferred_element_type=f32),
        arrived,
        bf16,
    ).astype(bf16)
    grad_bias = jnp.sum(lax.optimization_barrier(grad_pre).astype(f32), axis=0)
    bias_share = share_sum(lambda rows: rows, grad_bias, f32)
    dec_share = jnp.stack([part.T for part in dec_parts])[:, None]
    return (recon, enc_share[None], bias_share[None], dec_share, grad_b_dec)


MESH = pl.DeviceIdType.MESH
COPIES = 128


def rows_by_rows(left, right):
    return lax.dot_general(
        left, right, (((1,), (1,)), ((), ())), preferred_element_type=jnp.float32
    )


def step_kernel(
    expert_ids,
    slot_ids,
    live_mask,
    b_enc,
    b_dec,
    tokens,
    targets,
    w_enc,
    w_dec,
    recon_out,
    enc_out,
    bias_out,
    dec_out,
    bdec_out,
    ids_in,
    slot_in,
    live_in,
    b_enc_in,
    b_dec_in,
    tok_in,
    tok_t,
    goal_in,
    place,
    bias_pad,
    enc_wide,
    dec_wide,
    cells_near,
    cells_far,
    goal_out,
    alive_out,
    enc_in,
    enc_t,
    dec_in,
    dec_t,
    xin,
    goal,
    alive,
    latents,
    active,
    grad_lat,
    grad_pre,
    partial,
    first_x,
    first_y,
    next_x,
    next_y,
    last_x,
    last_y,
    errors,
    back_out,
    back_in,
    dec_sum,
    enc_sum,
    err_sum,
    err_came,
    err_all,
    send_sem,
    recv_sem,
    load_sem,
):
    f32, bf16 = jnp.float32, jnp.bfloat16
    layer = lax.axis_index("layer")
    expert = lax.axis_index("expert")
    core = lax.axis_index("dp")
    low, high = layer % 2, layer // 2
    beside_x = high * 2 + 1 - low
    beside_y = (1 - high) * 2 + low
    facing = 3 - layer
    along_x, along_y = {"layer": beside_x}, {"layer": beside_y}
    peers = {
        1: {"expert": expert + 1 - 2 * (expert % 2)},
        2: {"expert": (expert + 2) % 4},
        3: {"expert": 3 - expert},
    }
    twin = {"dp": 1 - core}

    tok_rows, width = tok_in.shape
    kinds = goal_in.shape[0]
    latent = enc_in.shape[1]
    count = place.shape[0]
    quarter = width // 4
    half = quarter // 2
    share = width // 2
    cap = count // 4
    coef = 2.0 / math.sqrt(tok_rows)

    def lanes(block):
        return pl.ds(block * 2 * cap, cap)

    def twin_lanes(block):
        return pl.ds(block * 2 * cap + cap, cap)

    def pair(block):
        return pl.ds(block * 2 * cap, 2 * cap)

    def slots(block):
        return pl.ds(block * cap, cap)

    def rows(start, size):
        return pl.ds(pl.multiple_of(start, 16), size)

    sends = []

    def send(source, target, device):
        number = len(sends)
        copy = pltpu.make_async_remote_copy(
            src_ref=source,
            dst_ref=target,
            send_sem=send_sem.at[number],
            recv_sem=recv_sem.at[number],
            device_id=device,
            device_id_type=MESH,
        )
        copy.start()
        sends.append(copy)
        return copy

    barrier = pltpu.get_barrier_semaphore()
    partners = [peers[1], peers[2], peers[3], along_x, along_y, twin]
    for partner in partners:
        pl.semaphore_signal(barrier, inc=1, device_id=partner, device_id_type=MESH)
    loads = [
        pltpu.make_async_copy(source, target, load_sem.at[number])
        for number, (source, target) in enumerate(
            [
                (expert_ids, ids_in),
                (slot_ids, slot_in),
                (tokens, tok_in),
                (b_enc, b_enc_in),
                (w_enc, enc_in),
                (w_dec, dec_in),
                (b_dec, b_dec_in),
                (live_mask, live_in),
                (targets, goal_in),
            ]
        )
    ]
    load_ids, load_slots, load_tokens, load_b_enc, load_enc = loads[:5]
    load_dec, load_b_dec, load_live, load_goal = loads[5:]
    for load in loads:
        load.start()

    own = rows(layer * quarter, quarter)
    other = rows(facing * quarter, quarter)
    step = 256

    load_ids.wait()
    load_slots.wait()
    cell = (ids_in[...] ^ expert) * cap + slot_in[...]
    marks = lax.broadcasted_iota(jnp.int32, (count, tok_rows), 0) == cell
    place[...] = jnp.where(marks, 1.0, 0.0).astype(bf16)
    load_tokens.wait()

    @pl.loop(0, width // step)
    def _(i):
        part = rows(i * step, step)
        tok_t[part, :] = tok_in[:, part].T

    @pl.loop(0, 4)
    def _(q):
        part = rows(q * quarter, quarter)
        moved = rows_by_rows(tok_t[part, :], place[: 2 * cap, :]).astype(bf16)
        xin[part, lanes(0)] = moved[:, :cap]
        cells_near[part, :] = moved[:, cap:]

    straight, across, flags, goals = {}, {}, {}, {}
    pl.semaphore_wait(barrier, len(partners))
    straight[1] = send(cells_near, xin.at[:, lanes(1)], peers[1])

    load_b_enc.wait()
    bias_pad[:, :latent] = jnp.broadcast_to(b_enc_in[...], (cap, latent))
    enc_wide[...] = bias_pad[:, :latent].T
    load_enc.wait()

    @pl.loop(0, width // step)
    def _(i):
        part = rows(i * step, step)
        enc_t[:, part] = enc_in[part, :].T

    def share_rows(ref, k, part):
        return send(ref.at[part, lanes(k)], ref.at[part, twin_lanes(k)], twin)

    theirs = rows((1 - core) * share, share)
    spread, traded = {}, {}

    def forward(k):
        straight[k].wait_recv()
        spread[k] = [
            send(xin.at[own, lanes(k)], xin.at[own, lanes(k)], along_x),
            send(xin.at[own, lanes(k)], xin.at[own, lanes(k)], along_y),
        ]

    def encode(k):
        if k == 1:
            straight[k].wait_recv()
        elif k:
            across[k].wait_recv()
            for copy in spread[k]:
                copy.wait_recv()

        @pl.loop(0, latent // step)
        def _(i):
            part = rows(i * step, step)
            pre = jnp.dot(enc_t[part, :], xin[:, lanes(k)], preferred_element_type=f32)
            value = jnp.maximum(pre + enc_wide[part, :], 0.0)
            active[part, slots(k)] = value
            latents[part, lanes(k)] = (value * value).astype(bf16)

    def trade(k):
        everything = rows(0, latent)
        traded[k] = [share_rows(latents, k, everything), share_rows(xin, k, theirs)]

    reduced = {}

    def decode(k, t):
        @pl.loop(0, 4)
        def _(q):
            product = jnp.dot(
                dec_t[t, rows(q * quarter, quarter), :],
                latents[:, lanes(k)],
                preferred_element_type=f32,
            ).astype(bf16)
            partial[k, t, q // 2, q % 2, 0] = product[:half]
            partial[k, t, q // 2, q % 2, 1] = product[half:]

        reduced[k, t] = [
            send(partial.at[k, t, :, 1 - low, 0], first_x.at[k, t], along_x),
            send(partial.at[k, t, 1 - high, :, 1], first_y.at[k, t], along_y),
        ]

    settled = {}

    def combine(k, t):
        for copy in reduced[k, t]:
            copy.wait_recv()
        next_y[k, t] = (
            partial[k, t, 1 - high, low, 0].astype(f32) + first_x[k, t, 1 - high].astype(f32)
        ).astype(bf16)
        next_x[k, t] = (
            partial[k, t, high, 1 - low, 1].astype(f32) + first_y[k, t, 1 - low].astype(f32)
        ).astype(bf16)
        settled[k, t] = [
            send(next_y.at[k, t], last_y.at[k, t], along_y),
            send(next_x.at[k, t], last_x.at[k, t], along_x),
        ]

    gathered, returned = {}, {}

    def judge(k, t):
        for copy in settled[k, t]:
            copy.wait_recv()
        if k and t == 0:
            flags[k].wait_recv()
            goals[k].wait_recv()
        scale = alive[0:1, slots(k)] * coef
        for h, (mine, late) in enumerate(
            ((first_x[k, t, high], last_y[k, t]), (first_y[k, t, low], last_x[k, t]))
        ):
            total = partial[k, t, high, low, h].astype(f32) + mine.astype(f32)
            total = (total + late.astype(f32)).astype(bf16).astype(f32)
            part = pl.ds(h * half, half)
            full = total + dec_wide[t, part, :]
            if k:
                back_out[k - 1, t, part, :] = full.astype(bf16)
            else:
                back_in[t, part, slots(0)] = full.astype(bf16)
            gap = full - goal[t, part, slots(k)].astype(f32)
            errors[t, rows(layer * quarter + h * half, half), lanes(k)] = (
                scale * gap
            ).astype(bf16)
        piece = errors.at[t, own, lanes(k)]
        gathered[k, t] = [send(piece, piece, along_x), send(piece, piece, along_y)]

    def give_back(k, t):
        returned[k, t] = send(back_out.at[k - 1, t], back_in.at[t, :, slots(k)], peers[k])

    relayed = {}

    def relay(k, t):
        for copy in gathered[k, t]:
            copy.wait_recv()
        from_x = errors.at[t, rows(beside_x * quarter, half), lanes(k)]
        from_y = errors.at[t, rows(beside_y * quarter + half, half), lanes(k)]
        relayed[k, t] = [send(from_x, from_x, along_y), send(from_y, from_y, along_x)]

    handed = {}

    def backward(k, t):
        for copy in relayed[k, t]:
            copy.wait_recv()
        handed[k, t] = share_rows(errors.at[t], k, theirs)

        @pl.loop(0, latent // step)
        def _(i):
            part = rows(i * step, step)
            value = jnp.dot(dec_in[t, part, :], errors[t, :, lanes(k)], preferred_element_type=f32)
            if t:
                value = value + grad_lat[part, :]
            if t < kinds - 1:
                grad_lat[part, :] = value
            else:
                grad_pre[part, lanes(k)] = (
                    value * (2.0 * active[part, slots(k)])
                ).astype(bf16)

        if t == kinds - 1:
            handed[k] = share_rows(grad_pre, k, rows(0, latent))

    third = share // 3
    final = 3

    def grow_dec(k, t):
        if t == 0:
            for copy in traded[k]:
                copy.wait_recv()
        handed[k, t].wait_recv()

        @pl.loop(0, 3)
        def _(j):
            part = pl.ds(pl.multiple_of(j * third, 128), third)
            value = rows_by_rows(
                latents[:, pair(k)], errors[t, rows(core * share + j * third, third), pair(k)]
            )
            if k:
                value = value + dec_sum[t, :, part]
            if k < final:
                dec_sum[t, :, part] = value
            else:
                dec_out[t, :, part] = value.astype(bf16)

    def grow_enc(k):
        handed[k].wait_recv()

        @pl.loop(0, 3)
        def _(j):
            part = rows(j * third, third)
            value = rows_by_rows(
                xin[rows(core * share + j * third, third), pair(k)], grad_pre[:, pair(k)]
            )
            if k:
                value = value + enc_sum[part, :]
            if k < final:
                enc_sum[part, :] = value
            else:
                enc_out[part, :] = value.astype(bf16)

    def each(stage, *key):
        for t in range(kinds):
            stage(*key, t)

    encode(0)
    load_dec.wait()
    for t in range(kinds):

        @pl.loop(0, width // step)
        def _(i):
            part = rows(i * step, step)
            dec_t[t, part, :] = dec_in[t, :, part].T

        decode(0, t)
    for number, part in enumerate((own, other)):
        cells_far[number] = rows_by_rows(tok_t[part, :], place[2 * cap :, :]).astype(bf16)
        for m in (2, 3):
            (across if number else straight)[m] = send(
                cells_far.at[number, :, slots(m - 2)], xin.at[part, lanes(m)], peers[m]
            )
    trade(0)

    load_goal.wait()
    load_live.wait()
    load_b_dec.wait()
    live = jnp.broadcast_to(live_in[...].astype(f32).astype(bf16), (8, tok_rows))
    shown = rows_by_rows(live, place[...])
    alive[:, slots(0)] = shown[:, :cap]
    alive_out[...] = shown[:, cap:]
    for t in range(kinds):
        moved = rows_by_rows(goal_in[t], place[...]).astype(bf16)
        goal[t, :, slots(0)] = moved[:, :cap]
        goal_out[t] = moved[:, cap:]
        bias_pad[:, :quarter] = jnp.broadcast_to(b_dec_in[t : t + 1, :], (cap, quarter))
        dec_wide[t] = bias_pad[...].T[:quarter]
    for m in (1, 2, 3):
        flags[m] = send(alive_out.at[:, slots(m - 1)], alive.at[:, slots(m)], peers[m])
        goals[m] = send(goal_out.at[:, :, slots(m - 1)], goal.at[:, :, slots(m)], peers[m])

    each(combine, 0)
    each(judge, 0)
    encode(1)
    each(decode, 1)
    trade(1)
    forward(2)
    each(relay, 0)
    forward(3)
    each(combine, 1)
    encode(2)
    each(decode, 2)
    trade(2)
    each(judge, 1)
    each(give_back, 1)
    each(backward, 0)
    each(combine, 2)
    each(relay, 1)
    encode(3)
    each(decode, 3)
    trade(3)
    each(judge, 2)
    each(give_back, 2)
    each(grow_dec, 0)
    grow_enc(0)
    each(backward, 1)
    each(combine, 3)
    each(relay, 2)
    each(grow_dec, 1)
    grow_enc(1)
    judge(3, 0)
    give_back(3, 0)
    judge(3, 1)
    ones = jnp.ones((8, cap), bf16)
    for t in range(kinds):
        err_sum[t] = sum(rows_by_rows(ones, errors[t, own, lanes(k)]) for k in range(4))
    err_swap = send(err_sum, err_came, twin)
    each(backward, 2)
    relay(3, 0)
    err_swap.wait_recv()
    err_all[expert] = err_sum[...] + err_came[...]
    err_spread = [send(err_all.at[expert], err_all.at[expert], peers[m]) for m in (1, 2, 3)]
    give_back(3, 1)
    relay(3, 1)
    each(grow_dec, 2)
    grow_enc(2)
    backward(3, 0)
    grow_dec(3, 0)
    for k in (1, 2, 3):
        returned[k, 0].wait_recv()

    def restore(t):
        recon_out[t] = jnp.dot(
            back_in[t], place[...], preferred_element_type=f32
        ).astype(bf16)

    restore(0)
    backward(3, 1)
    grow_dec(3, 1)
    grow_enc(3)
    side = latent // 2
    bias_out[...] = rows_by_rows(
        jnp.ones((8, 8 * cap), bf16), grad_pre[rows(core * side, side), :]
    )[0:1]
    for t in range(1, kinds):
        for k in (1, 2, 3):
            returned[k, t].wait_recv()
        restore(t)
    for copy in err_spread:
        copy.wait_recv()
    for t in range(kinds):
        total = err_all[0, t] + err_all[1, t] + err_all[2, t] + err_all[3, t]
        bdec_out[t : t + 1, :] = total[0:1]

    for copy in sends:
        copy.wait_send()


def store_kernel(*refs):
    sources, results, sem = refs[:5], refs[5:10], refs[10]
    copies = [
        pltpu.make_async_copy(source, result, sem.at[number])
        for number, (source, result) in enumerate(zip(sources, results))
    ]
    for copy in copies:
        copy.start()
    for copy in copies:
        copy.wait()


def local(tokens, expert_ids, slot_ids, live_mask, w_enc, b_enc, w_dec, b_dec, targets):
    f32, bf16 = jnp.float32, jnp.bfloat16
    n_expert = lax.axis_size("expert")
    n_layer = lax.axis_size("layer")
    assert lax.axis_size("dp") == 2
    if n_expert != 4 or n_layer != 4:
        return plain(
            tokens, expert_ids, slot_ids, live_mask, w_enc, b_enc, w_dec, b_dec, targets
        )
    tok_rows, width = tokens.shape
    cap = 2 * tok_rows // n_expert
    count = n_expert * cap
    quarter, share = width // 4, width // 2
    half = quarter // 2
    padded = -(-quarter // 128) * 128
    latent = w_enc.shape[2]
    kinds = w_dec.shape[0]
    rest = count - cap

    vmem = pl.BlockSpec(memory_space=pltpu.VMEM)
    hbm = pl.BlockSpec(memory_space=pl.ANY)
    scratch = [
        ((1, tok_rows), jnp.int32),
        ((1, tok_rows), jnp.int32),
        ((1, tok_rows), jnp.int32),
        ((1, latent), f32),
        ((kinds, quarter), f32),
        ((tok_rows, width), bf16),
        ((width, tok_rows), bf16),
        ((kinds, quarter, tok_rows), bf16),
        ((count, tok_rows), bf16),
        ((cap, max(padded, latent)), f32),
        ((latent, cap), f32),
        ((kinds, quarter, cap), f32),
        ((width, cap), bf16),
        ((2, quarter, rest - cap), bf16),
        ((kinds, quarter, rest), bf16),
        ((8, rest), f32),
        ((width, latent), bf16),
        ((latent, width), bf16),
        ((kinds, latent, width), bf16),
        ((kinds, width, latent), bf16),
        ((width, 2 * count), bf16),
        ((kinds, quarter, count), bf16),
        ((8, count), f32),
        ((latent, 2 * count), bf16),
        ((latent, count), f32),
        ((latent, cap), f32),
        ((latent, 2 * count), bf16),
        ((4, kinds, 2, 2, 2, half, cap), bf16),
        ((4, kinds, 2, half, cap), bf16),
        ((4, kinds, 2, half, cap), bf16),
        ((4, kinds, half, cap), bf16),
        ((4, kinds, half, cap), bf16),
        ((4, kinds, half, cap), bf16),
        ((4, kinds, half, cap), bf16),
        ((kinds, width, 2 * count), bf16),
        ((3, kinds, quarter, cap), bf16),
        ((kinds, quarter, count), bf16),
        ((kinds, latent, share), f32),
        ((share, latent), f32),
        ((kinds, 8, quarter), f32),
        ((kinds, 8, quarter), f32),
        ((4, kinds, 8, quarter), f32),
    ]
    results = [
        ((kinds, quarter, tok_rows), bf16),
        ((share, latent), bf16),
        ((1, latent // 2), f32),
        ((kinds, latent, share), bf16),
        ((kinds, quarter), f32),
    ]
    made = pl.pallas_call(
        step_kernel,
        out_shape=tuple(pltpu.VMEM(shape, dtype) for shape, dtype in results),
        in_specs=[hbm] * 9,
        out_specs=(vmem,) * 5,
        scratch_shapes=[pltpu.VMEM(shape, dtype) for shape, dtype in scratch]
        + [
            pltpu.SemaphoreType.DMA((COPIES,)),
            pltpu.SemaphoreType.DMA((COPIES,)),
            pltpu.SemaphoreType.DMA((9,)),
        ],
        compiler_params=pltpu.CompilerParams(
            collective_id=0, has_side_effects=True, vmem_limit_bytes=60 * 10**6
        ),
        name="step",
    )(
        expert_ids[None],
        slot_ids[None],
        live_mask[None],
        b_enc,
        b_dec,
        tokens,
        jnp.swapaxes(targets, 1, 2),
        w_enc[0],
        w_dec[:, 0],
    )
    recon, enc, bias, dec, bdec = pl.pallas_call(
        store_kernel,
        out_shape=tuple(jax.ShapeDtypeStruct(shape, dtype) for shape, dtype in results),
        in_specs=[vmem] * 5,
        out_specs=(hbm,) * 5,
        scratch_shapes=[pltpu.SemaphoreType.DMA((5,))],
        compiler_params=pltpu.CompilerParams(vmem_limit_bytes=2**20),
        name="store",
    )(*[pltpu.with_memory_space_constraint(value, pltpu.VMEM) for value in made])
    return (jnp.swapaxes(recon, 1, 2), enc[None], bias, dec[:, None], bdec)


def solution(mesh):
    placed = (
        P(("expert", "dp"), None),
        P(("expert", "dp")),
        P(("expert", "dp")),
        P(("expert", "dp")),
        P("expert", None, "layer"),
        P("expert", "layer"),
        P(None, "expert", "layer", None),
        P(None, "layer"),
        P(None, ("expert", "dp"), "layer"),
    )
    return jax.shard_map(
        local,
        mesh=mesh,
        in_specs=placed,
        out_specs=(
            P(None, ("expert", "dp"), "layer"),
            P("expert", "dp", "layer"),
            P("expert", ("layer", "dp")),
            P(None, "expert", "layer", "dp"),
            P(None, "layer"),
        ),
        check_vma=False,
    )
```

```python
import math

import jax
import jax.numpy as jnp
from jax import lax
from jax.experimental import pallas as pl
from jax.experimental.pallas import tpu as pltpu
from jax.sharding import PartitionSpec as P


def swap(values, mask, axis="layer"):
    size = lax.axis_size(axis)
    return lax.ppermute(values, axis, [(i, i ^ mask) for i in range(size)])


def exchange_experts(values):
    size = lax.axis_size("expert")
    if size != 4:
        return lax.all_to_all(values, "expert", split_axis=1, concat_axis=1, tiled=True)
    width = values.shape[1] // size
    blocks = [values[:, k * width : (k + 1) * width] for k in range(size)]
    for mask in (2, 3, 1):
        blocks[mask] = swap(blocks[mask], mask, "expert")
    return jnp.concatenate(blocks, axis=1)


def sum_all(values, axes):
    for axis in axes:
        size = lax.axis_size(axis)
        if size & (size - 1):
            values = lax.psum(values, axis)
            continue
        mask = 1
        while mask < size:
            values = values + swap(values, mask, axis)
            mask *= 2
    return values


def share_sum(product, rows, fills):
    depth = rows.shape[0] // 2
    me = lax.axis_index("dp")
    sent = product(lax.dynamic_slice_in_dim(rows, (1 - me) * depth, depth, 0))
    came = swap(sent.astype(fills), 1, "dp")
    own = product(lax.dynamic_slice_in_dim(rows, me * depth, depth, 0))
    return own + came.astype(jnp.float32)


def gather_layers(piece, beside=None):
    size = lax.axis_size("layer")
    if size != 4 or piece.shape[0] % 2:
        return lax.all_gather(piece, "layer", axis=0, tiled=True), beside
    me = lax.axis_index("layer")
    depth = piece.shape[0]
    half = depth // 2
    near = swap(piece, 1)
    far = swap(piece, 2)
    if beside is not None:
        near, far, beside = lax.optimization_barrier((near, far, beside))
    first = swap(far[:half], 1)
    second = swap(near[half:], 2)
    whole = jnp.zeros((size * depth,) + piece.shape[1:], piece.dtype)
    for offset, value in (
        (me * depth, piece),
        ((me ^ 1) * depth, near),
        ((me ^ 2) * depth, far),
        ((me ^ 3) * depth, first),
        ((me ^ 3) * depth + half, second),
    ):
        whole = lax.dynamic_update_slice_in_dim(whole, value, offset, 0)
    return whole, beside


def scatter_sum(values):
    size = lax.axis_size("layer")
    depth = values.shape[0] // size
    if size != 4 or depth % 2:
        return lax.psum_scatter(values, "layer", scatter_dimension=0, tiled=True)
    f32 = jnp.float32
    me = lax.axis_index("layer")
    low, high = me % 2, me // 2
    pieces = values.reshape((2, 2, 2, depth // 2) + values.shape[1:])

    def pick(array, index, axis):
        return lax.dynamic_index_in_dim(array, index, axis, keepdims=False)

    one, two = pieces[:, :, 0], pieces[:, :, 1]
    one_in = swap(pick(one, 1 - low, 1), 1)
    two_in = swap(pick(two, 1 - high, 0), 2)
    one_sum = pick(one, low, 1).astype(f32) + one_in.astype(f32)
    two_sum = pick(two, high, 0).astype(f32) + two_in.astype(f32)
    one_last = swap(pick(one_sum, 1 - high, 0).astype(values.dtype), 2)
    two_last = swap(pick(two_sum, 1 - low, 0).astype(values.dtype), 1)
    return jnp.concatenate(
        [
            (pick(one_sum, high, 0) + one_last.astype(f32)).astype(values.dtype),
            (pick(two_sum, low, 0) + two_last.astype(f32)).astype(values.dtype),
        ]
    )


def plain(tokens, expert_ids, slot_ids, live_mask, w_enc, b_enc, w_dec, b_dec, targets):
    f32, bf16 = jnp.float32, jnp.bfloat16
    n_expert = lax.axis_size("expert")
    n_layer = lax.axis_size("layer")
    assert lax.axis_size("dp") == 2
    tok_rows, model_width = tokens.shape
    capacity = 2 * tok_rows // n_expert
    total_cells = n_expert * capacity
    offset = lax.axis_index("expert") if n_expert == 4 else 0
    cell_index = (expert_ids ^ offset) * capacity + slot_ids
    quarter = model_width // n_layer
    targets_count = w_dec.shape[0]
    enc_weight = w_enc[0]
    place = (
        lax.broadcasted_iota(jnp.int32, (total_cells, tok_rows), 0) == cell_index[None, :]
    ).astype(bf16)

    cells = lax.dot_general(
        tokens, place, (((0,), (1,)), ((), ())), preferred_element_type=f32
    ).astype(bf16)
    own = lax.dynamic_slice_in_dim(cells, lax.axis_index("layer") * quarter, quarter, 0)
    arrived_part = exchange_experts(own)
    arrived, _ = gather_layers(arrived_part)
    pre_act = jnp.einsum("dr,dl->rl", arrived, enc_weight, preferred_element_type=f32)
    pre_act = pre_act + b_enc[0][None, :]
    active = jnp.maximum(pre_act, 0.0)
    latents = (active * active).astype(bf16)

    coef = 2.0 / math.sqrt(tok_rows)
    live_wide = live_mask.astype(f32)
    partials = [
        jnp.einsum("ld,rl->dr", w_dec[t, 0], latents, preferred_element_type=f32).astype(bf16)
        for t in range(targets_count)
    ]
    summed = [scatter_sum(p) for p in partials]
    recons, errors, parts = [], [], []
    for t in range(targets_count):
        returned = exchange_experts(summed[t])
        recon_sum = jnp.einsum("dr,ri->di", returned, place, preferred_element_type=f32)
        recon_full = recon_sum + b_dec[t][:, None]
        recons.append(recon_full.astype(bf16).T)
        error = (
            coef * live_wide[None, :] * (recon_full - targets[t].T.astype(f32))
        ).astype(bf16)
        errors.append(jnp.sum(error.astype(f32), axis=1))
        outgoing = jnp.einsum(
            "di,ri->dr", error, place, preferred_element_type=f32
        ).astype(bf16)
        parts.append(exchange_experts(outgoing))
    recon = jnp.stack(recons)
    grad_b_dec = sum_all(jnp.stack(errors), ("dp", "expert"))
    beside = parts[1:] + [None]
    segments = []
    for t in range(targets_count):
        segment, beside[t] = gather_layers(parts[t], beside[t])
        if t + 1 < targets_count:
            parts[t + 1] = beside[t]
        segments.append(segment)

    grad_lat = sum(
        jnp.einsum("dr,ld->rl", segments[t], w_dec[t, 0], preferred_element_type=f32)
        for t in range(targets_count)
    )
    dec_parts = [
        share_sum(
            lambda rows: jnp.einsum("dr,rl->dl", rows, latents, preferred_element_type=f32),
            segments[t],
            bf16,
        ).astype(bf16)
        for t in range(targets_count)
    ]
    grad_pre = (grad_lat * (2.0 * active)).astype(bf16)
    enc_share = share_sum(
        lambda rows: jnp.einsum("dr,rl->dl", rows, grad_pre, preferred_element_type=f32),
        arrived,
        bf16,
    ).astype(bf16)
    grad_bias = jnp.sum(lax.optimization_barrier(grad_pre).astype(f32), axis=0)
    bias_share = share_sum(lambda rows: rows, grad_bias, f32)
    dec_share = jnp.stack([part.T for part in dec_parts])[:, None]
    return (recon, enc_share[None], bias_share[None], dec_share, grad_b_dec)


MESH = pl.DeviceIdType.MESH
COPIES = 128


def rows_by_rows(left, right):
    return lax.dot_general(
        left, right, (((1,), (1,)), ((), ())), preferred_element_type=jnp.float32
    )


def step_kernel(
    expert_ids,
    slot_ids,
    live_mask,
    b_enc,
    b_dec,
    tokens,
    targets,
    w_enc,
    w_dec,
    recon_out,
    enc_out,
    bias_out,
    dec_out,
    bdec_out,
    ids_in,
    slot_in,
    live_in,
    b_enc_in,
    b_dec_in,
    tok_in,
    x_rows,
    goal_in,
    place,
    bias_pad,
    enc_wide,
    dec_wide,
    cells_near,
    cells_far,
    goal_out,
    alive_out,
    enc_in,
    enc_t,
    dec_in,
    dec_t,
    xin,
    goal,
    alive,
    latents,
    active,
    grad_lat,
    grad_pre,
    partial,
    first_x,
    first_y,
    next_x,
    next_y,
    last_x,
    last_y,
    errors,
    back_out,
    back_in,
    dec_sum,
    enc_sum,
    err_sum,
    err_came,
    err_all,
    send_sem,
    recv_sem,
    load_sem,
):
    f32, bf16 = jnp.float32, jnp.bfloat16
    layer = lax.axis_index("layer")
    expert = lax.axis_index("expert")
    core = lax.axis_index("dp")
    low, high = layer % 2, layer // 2
    beside_x = high * 2 + 1 - low
    beside_y = (1 - high) * 2 + low
    facing = 3 - layer
    along_x, along_y = {"layer": beside_x}, {"layer": beside_y}
    peers = {
        1: {"expert": expert + 1 - 2 * (expert % 2)},
        2: {"expert": (expert + 2) % 4},
        3: {"expert": 3 - expert},
    }
    twin = {"dp": 1 - core}

    tok_rows, width = tok_in.shape
    kinds = goal_in.shape[0]
    latent = enc_in.shape[1]
    count = place.shape[0]
    quarter = width // 4
    half = quarter // 2
    share = width // 2
    cap = count // 4
    coef = 2.0 / math.sqrt(tok_rows)

    def lanes(block):
        return pl.ds(block * 2 * cap, cap)

    def twin_lanes(block):
        return pl.ds(block * 2 * cap + cap, cap)

    def pair(block):
        return pl.ds(block * 2 * cap, 2 * cap)

    def slots(block):
        return pl.ds(block * cap, cap)

    def rows(start, size):
        return pl.ds(pl.multiple_of(start, 16), size)

    sends = []

    def send(source, target, device):
        number = len(sends)
        copy = pltpu.make_async_remote_copy(
            src_ref=source,
            dst_ref=target,
            send_sem=send_sem.at[number],
            recv_sem=recv_sem.at[number],
            device_id=device,
            device_id_type=MESH,
        )
        copy.start()
        sends.append(copy)
        return copy

    barrier = pltpu.get_barrier_semaphore()
    partners = [peers[1], peers[2], peers[3], along_x, along_y, twin]
    for partner in partners:
        pl.semaphore_signal(barrier, inc=1, device_id=partner, device_id_type=MESH)
    loads = [
        pltpu.make_async_copy(source, target, load_sem.at[number])
        for number, (source, target) in enumerate(
            [
                (expert_ids, ids_in),
                (slot_ids, slot_in),
                (tokens, tok_in),
                (b_enc, b_enc_in),
                (w_enc, enc_in),
                (w_dec, dec_in),
                (b_dec, b_dec_in),
                (live_mask, live_in),
                (targets, goal_in),
            ]
        )
    ]
    load_ids, load_slots, load_tokens, load_b_enc, load_enc = loads[:5]
    load_dec, load_b_dec, load_live, load_goal = loads[5:]
    for load in loads:
        load.start()

    own = rows(layer * quarter, quarter)
    other = rows(facing * quarter, quarter)
    step = 256
    wide = width // 3

    load_ids.wait()
    load_slots.wait()
    cell = (ids_in[...] ^ expert) * cap + slot_in[...]
    marks = lax.broadcasted_iota(jnp.int32, (count, tok_rows), 0) == cell
    place[...] = jnp.where(marks, 1.0, 0.0).astype(bf16)
    load_tokens.wait()

    @pl.loop(0, 3)
    def _(i):
        part = rows(i * wide, wide)
        moved = jnp.dot(
            place[: 2 * cap, :], tok_in[:, part], preferred_element_type=f32
        ).astype(bf16)
        x_rows[:, part] = moved[:cap]
        turned = moved.T
        xin[part, lanes(0)] = turned[:, :cap]
        cells_near[part, :] = turned[:, cap:]

    straight, across, flags, goals = {}, {}, {}, {}
    pl.semaphore_wait(barrier, len(partners))
    straight[1] = send(cells_near, xin.at[:, lanes(1)], peers[1])
    load_b_enc.wait()
    load_enc.wait()

    @pl.loop(0, latent // step)
    def _(i):
        part = rows(i * step, step)
        pre = jnp.dot(x_rows[...], enc_in[:, part], preferred_element_type=f32)
        value = jnp.maximum(pre + b_enc_in[:, part], 0.0)
        active[part, slots(0)] = value.T
        latents[part, lanes(0)] = (value * value).astype(bf16).T

    def share_rows(ref, k, part):
        return send(ref.at[part, lanes(k)], ref.at[part, twin_lanes(k)], twin)

    theirs = rows((1 - core) * share, share)
    spread, traded = {}, {}

    def forward(k):
        straight[k].wait_recv()
        spread[k] = [
            send(xin.at[own, lanes(k)], xin.at[own, lanes(k)], along_x),
            send(xin.at[own, lanes(k)], xin.at[own, lanes(k)], along_y),
        ]

    def encode(k):
        if k == 1:
            straight[k].wait_recv()
        else:
            across[k].wait_recv()
            for copy in spread[k]:
                copy.wait_recv()

        @pl.loop(0, latent // step)
        def _(i):
            part = rows(i * step, step)
            pre = jnp.dot(enc_t[part, :], xin[:, lanes(k)], preferred_element_type=f32)
            value = jnp.maximum(pre + enc_wide[part, :], 0.0)
            active[part, slots(k)] = value
            latents[part, lanes(k)] = (value * value).astype(bf16)

    def trade(k):
        everything = rows(0, latent)
        traded[k] = [share_rows(latents, k, everything), share_rows(xin, k, theirs)]

    reduced = {}

    def decode(k, t):
        @pl.loop(0, 4)
        def _(q):
            product = jnp.dot(
                dec_t[t, rows(q * quarter, quarter), :],
                latents[:, lanes(k)],
                preferred_element_type=f32,
            ).astype(bf16)
            partial[k, t, q // 2, q % 2, 0] = product[:half]
            partial[k, t, q // 2, q % 2, 1] = product[half:]

        reduced[k, t] = [
            send(partial.at[k, t, :, 1 - low, 0], first_x.at[k, t], along_x),
            send(partial.at[k, t, 1 - high, :, 1], first_y.at[k, t], along_y),
        ]

    settled = {}

    def combine(k, t):
        for copy in reduced[k, t]:
            copy.wait_recv()
        next_y[k, t] = (
            partial[k, t, 1 - high, low, 0].astype(f32) + first_x[k, t, 1 - high].astype(f32)
        ).astype(bf16)
        next_x[k, t] = (
            partial[k, t, high, 1 - low, 1].astype(f32) + first_y[k, t, 1 - low].astype(f32)
        ).astype(bf16)
        settled[k, t] = [
            send(next_y.at[k, t], last_y.at[k, t], along_y),
            send(next_x.at[k, t], last_x.at[k, t], along_x),
        ]

    gathered, returned = {}, {}

    def judge(k, t):
        for copy in settled[k, t]:
            copy.wait_recv()
        if k and t == 0:
            flags[k].wait_recv()
            goals[k].wait_recv()
        scale = alive[0:1, slots(k)] * coef
        for h, (mine, late) in enumerate(
            ((first_x[k, t, high], last_y[k, t]), (first_y[k, t, low], last_x[k, t]))
        ):
            total = partial[k, t, high, low, h].astype(f32) + mine.astype(f32)
            total = (total + late.astype(f32)).astype(bf16).astype(f32)
            part = pl.ds(h * half, half)
            full = total + dec_wide[t, part, :]
            if k:
                back_out[k - 1, t, part, :] = full.astype(bf16)
            else:
                back_in[t, part, slots(0)] = full.astype(bf16)
            gap = full - goal[t, part, slots(k)].astype(f32)
            errors[t, rows(layer * quarter + h * half, half), lanes(k)] = (
                scale * gap
            ).astype(bf16)
        piece = errors.at[t, own, lanes(k)]
        gathered[k, t] = [send(piece, piece, along_x), send(piece, piece, along_y)]

    def give_back(k, t):
        returned[k, t] = send(back_out.at[k - 1, t], back_in.at[t, :, slots(k)], peers[k])

    relayed = {}

    def relay(k, t):
        for copy in gathered[k, t]:
            copy.wait_recv()
        from_x = errors.at[t, rows(beside_x * quarter, half), lanes(k)]
        from_y = errors.at[t, rows(beside_y * quarter + half, half), lanes(k)]
        relayed[k, t] = [send(from_x, from_x, along_y), send(from_y, from_y, along_x)]

    handed = {}

    def backward(k, t):
        for copy in relayed[k, t]:
            copy.wait_recv()
        handed[k, t] = share_rows(errors.at[t], k, theirs)

        @pl.loop(0, latent // step)
        def _(i):
            part = rows(i * step, step)
            value = jnp.dot(dec_in[t, part, :], errors[t, :, lanes(k)], preferred_element_type=f32)
            if t:
                value = value + grad_lat[part, :]
            if t < kinds - 1:
                grad_lat[part, :] = value
            else:
                grad_pre[part, lanes(k)] = (
                    value * (2.0 * active[part, slots(k)])
                ).astype(bf16)

        if t == kinds - 1:
            handed[k] = share_rows(grad_pre, k, rows(0, latent))

    third = share // 3
    final = 3

    def grow_dec(k, t):
        if t == 0:
            for copy in traded[k]:
                copy.wait_recv()
        handed[k, t].wait_recv()

        @pl.loop(0, 3)
        def _(j):
            part = pl.ds(pl.multiple_of(j * third, 128), third)
            value = rows_by_rows(
                latents[:, pair(k)], errors[t, rows(core * share + j * third, third), pair(k)]
            )
            if k:
                value = value + dec_sum[t, :, part]
            if k < final:
                dec_sum[t, :, part] = value
            else:
                dec_out[t, :, part] = value.astype(bf16)

    def grow_enc(k):
        handed[k].wait_recv()

        @pl.loop(0, 3)
        def _(j):
            part = rows(j * third, third)
            value = rows_by_rows(
                xin[rows(core * share + j * third, third), pair(k)], grad_pre[:, pair(k)]
            )
            if k:
                value = value + enc_sum[part, :]
            if k < final:
                enc_sum[part, :] = value
            else:
                enc_out[part, :] = value.astype(bf16)

    def each(stage, *key):
        for t in range(kinds):
            stage(*key, t)

    load_dec.wait()
    for t in range(kinds):

        @pl.loop(0, width // step)
        def _(i):
            part = rows(i * step, step)
            dec_t[t, part, :] = dec_in[t, :, part].T

        decode(0, t)

    @pl.loop(0, 3)
    def _(i):
        part = rows(i * wide, wide)
        moved = jnp.dot(
            place[2 * cap :, :], tok_in[:, part], preferred_element_type=f32
        ).astype(bf16)
        cells_far[part, :] = moved.T

    for m in (2, 3):
        straight[m] = send(cells_far.at[own, slots(m - 2)], xin.at[own, lanes(m)], peers[m])
    for m in (2, 3):
        across[m] = send(cells_far.at[other, slots(m - 2)], xin.at[other, lanes(m)], peers[m])
    trade(0)

    load_goal.wait()
    load_live.wait()
    load_b_dec.wait()
    live = jnp.broadcast_to(live_in[...].astype(f32).astype(bf16), (8, tok_rows))
    shown = rows_by_rows(live, place[...])
    alive[:, slots(0)] = shown[:, :cap]
    alive_out[...] = shown[:, cap:]
    for t in range(kinds):
        moved = rows_by_rows(goal_in[t], place[...]).astype(bf16)
        goal[t, :, slots(0)] = moved[:, :cap]
        goal_out[t] = moved[:, cap:]
        bias_pad[:, :quarter] = jnp.broadcast_to(b_dec_in[t : t + 1, :], (cap, quarter))
        dec_wide[t] = bias_pad[...].T[:quarter]
    for m in (1, 2, 3):
        flags[m] = send(alive_out.at[:, slots(m - 1)], alive.at[:, slots(m)], peers[m])
        goals[m] = send(goal_out.at[:, :, slots(m - 1)], goal.at[:, :, slots(m)], peers[m])

    each(combine, 0)
    bias_pad[:, :latent] = jnp.broadcast_to(b_enc_in[...], (cap, latent))
    enc_wide[...] = bias_pad[:, :latent].T

    @pl.loop(0, width // step)
    def _(i):
        part = rows(i * step, step)
        enc_t[:, part] = enc_in[part, :].T

    each(judge, 0)
    encode(1)
    each(decode, 1)
    trade(1)
    forward(2)
    each(relay, 0)
    forward(3)
    each(combine, 1)
    encode(2)
    each(decode, 2)
    trade(2)
    each(judge, 1)
    each(give_back, 1)
    each(combine, 2)
    each(backward, 0)
    each(relay, 1)
    encode(3)
    each(decode, 3)
    trade(3)
    each(judge, 2)
    each(give_back, 2)
    each(grow_dec, 0)
    grow_enc(0)
    each(combine, 3)
    each(backward, 1)
    each(relay, 2)
    for t in range(kinds):
        judge(3, t)
        give_back(3, t)
    ones = jnp.ones((8, cap), bf16)
    for t in range(kinds):
        err_sum[t] = sum(rows_by_rows(ones, errors[t, own, lanes(k)]) for k in range(4))
    err_swap = send(err_sum, err_came, twin)
    each(grow_dec, 1)
    grow_enc(1)
    err_swap.wait_recv()
    err_all[expert] = err_sum[...] + err_came[...]
    err_spread = [send(err_all.at[expert], err_all.at[expert], peers[m]) for m in (1, 2, 3)]
    for t in range(kinds):
        backward(2, t)
        relay(3, t)
    each(grow_dec, 2)
    grow_enc(2)
    backward(3, 0)
    grow_dec(3, 0)
    for k in (1, 2, 3):
        returned[k, 0].wait_recv()

    def restore(t):
        recon_out[t] = jnp.dot(
            back_in[t], place[...], preferred_element_type=f32
        ).astype(bf16)

    restore(0)
    backward(3, 1)
    grow_dec(3, 1)
    grow_enc(3)
    side = latent // 2
    bias_out[...] = rows_by_rows(
        jnp.ones((8, 8 * cap), bf16), grad_pre[rows(core * side, side), :]
    )[0:1]
    for t in range(1, kinds):
        for k in (1, 2, 3):
            returned[k, t].wait_recv()
        restore(t)
    for copy in err_spread:
        copy.wait_recv()
    for t in range(kinds):
        total = err_all[0, t] + err_all[1, t] + err_all[2, t] + err_all[3, t]
        bdec_out[t : t + 1, :] = total[0:1]

    for copy in sends:
        copy.wait_send()


def store_kernel(*refs):
    sources, results, sem = refs[:5], refs[5:10], refs[10]
    copies = [
        pltpu.make_async_copy(source, result, sem.at[number])
        for number, (source, result) in enumerate(zip(sources, results))
    ]
    for copy in copies:
        copy.start()
    for copy in copies:
        copy.wait()


def local(tokens, expert_ids, slot_ids, live_mask, w_enc, b_enc, w_dec, b_dec, targets):
    f32, bf16 = jnp.float32, jnp.bfloat16
    n_expert = lax.axis_size("expert")
    n_layer = lax.axis_size("layer")
    assert lax.axis_size("dp") == 2
    if n_expert != 4 or n_layer != 4:
        return plain(
            tokens, expert_ids, slot_ids, live_mask, w_enc, b_enc, w_dec, b_dec, targets
        )
    tok_rows, width = tokens.shape
    cap = 2 * tok_rows // n_expert
    count = n_expert * cap
    quarter, share = width // 4, width // 2
    half = quarter // 2
    padded = -(-quarter // 128) * 128
    latent = w_enc.shape[2]
    kinds = w_dec.shape[0]
    rest = count - cap

    vmem = pl.BlockSpec(memory_space=pltpu.VMEM)
    hbm = pl.BlockSpec(memory_space=pl.ANY)
    scratch = [
        ((1, tok_rows), jnp.int32),
        ((1, tok_rows), jnp.int32),
        ((1, tok_rows), jnp.int32),
        ((1, latent), f32),
        ((kinds, quarter), f32),
        ((tok_rows, width), bf16),
        ((cap, width), bf16),
        ((kinds, quarter, tok_rows), bf16),
        ((count, tok_rows), bf16),
        ((cap, max(padded, latent)), f32),
        ((latent, cap), f32),
        ((kinds, quarter, cap), f32),
        ((width, cap), bf16),
        ((width, rest - cap), bf16),
        ((kinds, quarter, rest), bf16),
        ((8, rest), f32),
        ((width, latent), bf16),
        ((latent, width), bf16),
        ((kinds, latent, width), bf16),
        ((kinds, width, latent), bf16),
        ((width, 2 * count), bf16),
        ((kinds, quarter, count), bf16),
        ((8, count), f32),
        ((latent, 2 * count), bf16),
        ((latent, count), f32),
        ((latent, cap), f32),
        ((latent, 2 * count), bf16),
        ((4, kinds, 2, 2, 2, half, cap), bf16),
        ((4, kinds, 2, half, cap), bf16),
        ((4, kinds, 2, half, cap), bf16),
        ((4, kinds, half, cap), bf16),
        ((4, kinds, half, cap), bf16),
        ((4, kinds, half, cap), bf16),
        ((4, kinds, half, cap), bf16),
        ((kinds, width, 2 * count), bf16),
        ((3, kinds, quarter, cap), bf16),
        ((kinds, quarter, count), bf16),
        ((kinds, latent, share), f32),
        ((share, latent), f32),
        ((kinds, 8, quarter), f32),
        ((kinds, 8, quarter), f32),
        ((4, kinds, 8, quarter), f32),
    ]
    results = [
        ((kinds, quarter, tok_rows), bf16),
        ((share, latent), bf16),
        ((1, latent // 2), f32),
        ((kinds, latent, share), bf16),
        ((kinds, quarter), f32),
    ]
    made = pl.pallas_call(
        step_kernel,
        out_shape=tuple(pltpu.VMEM(shape, dtype) for shape, dtype in results),
        in_specs=[hbm] * 9,
        out_specs=(vmem,) * 5,
        scratch_shapes=[pltpu.VMEM(shape, dtype) for shape, dtype in scratch]
        + [
            pltpu.SemaphoreType.DMA((COPIES,)),
            pltpu.SemaphoreType.DMA((COPIES,)),
            pltpu.SemaphoreType.DMA((9,)),
        ],
        compiler_params=pltpu.CompilerParams(
            collective_id=0, has_side_effects=True, vmem_limit_bytes=60 * 10**6
        ),
        name="step",
    )(
        expert_ids[None],
        slot_ids[None],
        live_mask[None],
        b_enc,
        b_dec,
        tokens,
        jnp.swapaxes(targets, 1, 2),
        w_enc[0],
        w_dec[:, 0],
    )
    recon, enc, bias, dec, bdec = pl.pallas_call(
        store_kernel,
        out_shape=tuple(jax.ShapeDtypeStruct(shape, dtype) for shape, dtype in results),
        in_specs=[vmem] * 5,
        out_specs=(hbm,) * 5,
        scratch_shapes=[pltpu.SemaphoreType.DMA((5,))],
        compiler_params=pltpu.CompilerParams(vmem_limit_bytes=2**20),
        name="store",
    )(*[pltpu.with_memory_space_constraint(value, pltpu.VMEM) for value in made])
    return (jnp.swapaxes(recon, 1, 2), enc[None], bias, dec[:, None], bdec)


def solution(mesh):
    placed = (
        P(("expert", "dp"), None),
        P(("expert", "dp")),
        P(("expert", "dp")),
        P(("expert", "dp")),
        P("expert", None, "layer"),
        P("expert", "layer"),
        P(None, "expert", "layer", None),
        P(None, "layer"),
        P(None, ("expert", "dp"), "layer"),
    )
    return jax.shard_map(
        local,
        mesh=mesh,
        in_specs=placed,
        out_specs=(
            P(None, ("expert", "dp"), "layer"),
            P("expert", "dp", "layer"),
            P("expert", ("layer", "dp")),
            P(None, "expert", "layer", "dp"),
            P(None, "layer"),
        ),
        check_vma=False,
    )
```

```python
import math

import jax
import jax.numpy as jnp
from jax import lax
from jax.experimental import pallas as pl
from jax.experimental.pallas import tpu as pltpu
from jax.sharding import PartitionSpec as P


def swap(values, mask, axis="layer"):
    size = lax.axis_size(axis)
    return lax.ppermute(values, axis, [(i, i ^ mask) for i in range(size)])


def exchange_experts(values):
    size = lax.axis_size("expert")
    if size != 4:
        return lax.all_to_all(values, "expert", split_axis=1, concat_axis=1, tiled=True)
    width = values.shape[1] // size
    blocks = [values[:, k * width : (k + 1) * width] for k in range(size)]
    for mask in (2, 3, 1):
        blocks[mask] = swap(blocks[mask], mask, "expert")
    return jnp.concatenate(blocks, axis=1)


def sum_all(values, axes):
    for axis in axes:
        size = lax.axis_size(axis)
        if size & (size - 1):
            values = lax.psum(values, axis)
            continue
        mask = 1
        while mask < size:
            values = values + swap(values, mask, axis)
            mask *= 2
    return values


def share_sum(product, rows, fills):
    depth = rows.shape[0] // 2
    me = lax.axis_index("dp")
    sent = product(lax.dynamic_slice_in_dim(rows, (1 - me) * depth, depth, 0))
    came = swap(sent.astype(fills), 1, "dp")
    own = product(lax.dynamic_slice_in_dim(rows, me * depth, depth, 0))
    return own + came.astype(jnp.float32)


def gather_layers(piece, beside=None):
    size = lax.axis_size("layer")
    if size != 4 or piece.shape[0] % 2:
        return lax.all_gather(piece, "layer", axis=0, tiled=True), beside
    me = lax.axis_index("layer")
    depth = piece.shape[0]
    half = depth // 2
    near = swap(piece, 1)
    far = swap(piece, 2)
    if beside is not None:
        near, far, beside = lax.optimization_barrier((near, far, beside))
    first = swap(far[:half], 1)
    second = swap(near[half:], 2)
    whole = jnp.zeros((size * depth,) + piece.shape[1:], piece.dtype)
    for offset, value in (
        (me * depth, piece),
        ((me ^ 1) * depth, near),
        ((me ^ 2) * depth, far),
        ((me ^ 3) * depth, first),
        ((me ^ 3) * depth + half, second),
    ):
        whole = lax.dynamic_update_slice_in_dim(whole, value, offset, 0)
    return whole, beside


def scatter_sum(values):
    size = lax.axis_size("layer")
    depth = values.shape[0] // size
    if size != 4 or depth % 2:
        return lax.psum_scatter(values, "layer", scatter_dimension=0, tiled=True)
    f32 = jnp.float32
    me = lax.axis_index("layer")
    low, high = me % 2, me // 2
    pieces = values.reshape((2, 2, 2, depth // 2) + values.shape[1:])

    def pick(array, index, axis):
        return lax.dynamic_index_in_dim(array, index, axis, keepdims=False)

    one, two = pieces[:, :, 0], pieces[:, :, 1]
    one_in = swap(pick(one, 1 - low, 1), 1)
    two_in = swap(pick(two, 1 - high, 0), 2)
    one_sum = pick(one, low, 1).astype(f32) + one_in.astype(f32)
    two_sum = pick(two, high, 0).astype(f32) + two_in.astype(f32)
    one_last = swap(pick(one_sum, 1 - high, 0).astype(values.dtype), 2)
    two_last = swap(pick(two_sum, 1 - low, 0).astype(values.dtype), 1)
    return jnp.concatenate(
        [
            (pick(one_sum, high, 0) + one_last.astype(f32)).astype(values.dtype),
            (pick(two_sum, low, 0) + two_last.astype(f32)).astype(values.dtype),
        ]
    )


def plain(tokens, expert_ids, slot_ids, live_mask, w_enc, b_enc, w_dec, b_dec, targets):
    f32, bf16 = jnp.float32, jnp.bfloat16
    n_expert = lax.axis_size("expert")
    n_layer = lax.axis_size("layer")
    assert lax.axis_size("dp") == 2
    tok_rows, model_width = tokens.shape
    capacity = 2 * tok_rows // n_expert
    total_cells = n_expert * capacity
    offset = lax.axis_index("expert") if n_expert == 4 else 0
    cell_index = (expert_ids ^ offset) * capacity + slot_ids
    quarter = model_width // n_layer
    targets_count = w_dec.shape[0]
    enc_weight = w_enc[0]
    place = (
        lax.broadcasted_iota(jnp.int32, (total_cells, tok_rows), 0) == cell_index[None, :]
    ).astype(bf16)

    cells = lax.dot_general(
        tokens, place, (((0,), (1,)), ((), ())), preferred_element_type=f32
    ).astype(bf16)
    own = lax.dynamic_slice_in_dim(cells, lax.axis_index("layer") * quarter, quarter, 0)
    arrived_part = exchange_experts(own)
    arrived, _ = gather_layers(arrived_part)
    pre_act = jnp.einsum("dr,dl->rl", arrived, enc_weight, preferred_element_type=f32)
    pre_act = pre_act + b_enc[0][None, :]
    active = jnp.maximum(pre_act, 0.0)
    latents = (active * active).astype(bf16)

    coef = 2.0 / math.sqrt(tok_rows)
    live_wide = live_mask.astype(f32)
    partials = [
        jnp.einsum("ld,rl->dr", w_dec[t, 0], latents, preferred_element_type=f32).astype(bf16)
        for t in range(targets_count)
    ]
    summed = [scatter_sum(p) for p in partials]
    recons, errors, parts = [], [], []
    for t in range(targets_count):
        returned = exchange_experts(summed[t])
        recon_sum = jnp.einsum("dr,ri->di", returned, place, preferred_element_type=f32)
        recon_full = recon_sum + b_dec[t][:, None]
        recons.append(recon_full.astype(bf16).T)
        error = (
            coef * live_wide[None, :] * (recon_full - targets[t].T.astype(f32))
        ).astype(bf16)
        errors.append(jnp.sum(error.astype(f32), axis=1))
        outgoing = jnp.einsum(
            "di,ri->dr", error, place, preferred_element_type=f32
        ).astype(bf16)
        parts.append(exchange_experts(outgoing))
    recon = jnp.stack(recons)
    grad_b_dec = sum_all(jnp.stack(errors), ("dp", "expert"))
    beside = parts[1:] + [None]
    segments = []
    for t in range(targets_count):
        segment, beside[t] = gather_layers(parts[t], beside[t])
        if t + 1 < targets_count:
            parts[t + 1] = beside[t]
        segments.append(segment)

    grad_lat = sum(
        jnp.einsum("dr,ld->rl", segments[t], w_dec[t, 0], preferred_element_type=f32)
        for t in range(targets_count)
    )
    dec_parts = [
        share_sum(
            lambda rows: jnp.einsum("dr,rl->dl", rows, latents, preferred_element_type=f32),
            segments[t],
            bf16,
        ).astype(bf16)
        for t in range(targets_count)
    ]
    grad_pre = (grad_lat * (2.0 * active)).astype(bf16)
    enc_share = share_sum(
        lambda rows: jnp.einsum("dr,rl->dl", rows, grad_pre, preferred_element_type=f32),
        arrived,
        bf16,
    ).astype(bf16)
    grad_bias = jnp.sum(lax.optimization_barrier(grad_pre).astype(f32), axis=0)
    bias_share = share_sum(lambda rows: rows, grad_bias, f32)
    dec_share = jnp.stack([part.T for part in dec_parts])[:, None]
    return (recon, enc_share[None], bias_share[None], dec_share, grad_b_dec)


MESH = pl.DeviceIdType.MESH
COPIES = 128


def rows_by_rows(left, right):
    return lax.dot_general(
        left, right, (((1,), (1,)), ((), ())), preferred_element_type=jnp.float32
    )


def step_kernel(
    expert_ids,
    slot_ids,
    live_mask,
    b_enc,
    b_dec,
    tokens,
    targets,
    w_enc,
    w_dec,
    recon_out,
    enc_out,
    bias_out,
    dec_out,
    bdec_out,
    ids_in,
    slot_in,
    live_in,
    b_enc_in,
    b_dec_in,
    tok_in,
    x_rows,
    goal_in,
    place,
    bias_pad,
    enc_wide,
    dec_wide,
    cells_near,
    cells_far,
    goal_out,
    alive_out,
    enc_in,
    enc_t,
    dec_in,
    dec_t,
    xin,
    goal,
    alive,
    latents,
    active,
    grad_lat,
    grad_pre,
    partial,
    first_x,
    first_y,
    next_x,
    next_y,
    last_x,
    last_y,
    errors,
    back_out,
    back_in,
    dec_sum,
    enc_sum,
    err_sum,
    err_came,
    err_all,
    send_sem,
    recv_sem,
    load_sem,
):
    f32, bf16 = jnp.float32, jnp.bfloat16
    layer = lax.axis_index("layer")
    expert = lax.axis_index("expert")
    core = lax.axis_index("dp")
    low, high = layer % 2, layer // 2
    beside_x = high * 2 + 1 - low
    beside_y = (1 - high) * 2 + low
    facing = 3 - layer
    along_x, along_y = {"layer": beside_x}, {"layer": beside_y}
    peers = {
        1: {"expert": expert + 1 - 2 * (expert % 2)},
        2: {"expert": (expert + 2) % 4},
        3: {"expert": 3 - expert},
    }
    twin = {"dp": 1 - core}

    tok_rows, width = tok_in.shape
    kinds = goal_in.shape[0]
    latent = enc_in.shape[1]
    count = place.shape[0]
    quarter = width // 4
    half = quarter // 2
    share = width // 2
    cap = count // 4
    coef = 2.0 / math.sqrt(tok_rows)

    def lanes(block):
        return pl.ds(block * 2 * cap, cap)

    def twin_lanes(block):
        return pl.ds(block * 2 * cap + cap, cap)

    def pair(block):
        return pl.ds(block * 2 * cap, 2 * cap)

    def slots(block):
        return pl.ds(block * cap, cap)

    def rows(start, size):
        return pl.ds(pl.multiple_of(start, 16), size)

    sends = []

    def send(source, target, device):
        number = len(sends)
        copy = pltpu.make_async_remote_copy(
            src_ref=source,
            dst_ref=target,
            send_sem=send_sem.at[number],
            recv_sem=recv_sem.at[number],
            device_id=device,
            device_id_type=MESH,
        )
        copy.start()
        sends.append(copy)
        return copy

    barrier = pltpu.get_barrier_semaphore()
    partners = [peers[1], peers[2], peers[3], along_x, along_y, twin]
    for partner in partners:
        pl.semaphore_signal(barrier, inc=1, device_id=partner, device_id_type=MESH)
    loads = [
        pltpu.make_async_copy(source, target, load_sem.at[number])
        for number, (source, target) in enumerate(
            [
                (expert_ids, ids_in),
                (slot_ids, slot_in),
                (tokens, tok_in),
                (b_enc, b_enc_in),
                (w_enc, enc_in),
                (w_dec, dec_in),
                (b_dec, b_dec_in),
                (live_mask, live_in),
                (targets, goal_in),
            ]
        )
    ]
    load_ids, load_slots, load_tokens, load_b_enc, load_enc = loads[:5]
    load_dec, load_b_dec, load_live, load_goal = loads[5:]
    for load in loads:
        load.start()

    own = rows(layer * quarter, quarter)
    other = rows(facing * quarter, quarter)
    step = 256
    wide = width // 3

    load_ids.wait()
    load_slots.wait()
    cell = (ids_in[...] ^ expert) * cap + slot_in[...]
    marks = lax.broadcasted_iota(jnp.int32, (count, tok_rows), 0) == cell
    place[...] = jnp.where(marks, 1.0, 0.0).astype(bf16)
    load_tokens.wait()

    @pl.loop(0, 3)
    def _(i):
        part = rows(i * wide, wide)
        moved = jnp.dot(
            place[: 2 * cap, :], tok_in[:, part], preferred_element_type=f32
        ).astype(bf16)
        x_rows[:, part] = moved[:cap]
        turned = moved.T
        xin[part, lanes(0)] = turned[:, :cap]
        cells_near[part, :] = turned[:, cap:]

    straight, across, flags, goals = {}, {}, {}, {}
    pl.semaphore_wait(barrier, len(partners))
    straight[1] = send(cells_near, xin.at[:, lanes(1)], peers[1])
    load_b_enc.wait()
    load_enc.wait()

    @pl.loop(0, latent // step)
    def _(i):
        part = rows(i * step, step)
        pre = jnp.dot(x_rows[...], enc_in[:, part], preferred_element_type=f32)
        value = jnp.maximum(pre + b_enc_in[:, part], 0.0)
        active[part, slots(0)] = value.T
        latents[part, lanes(0)] = (value * value).astype(bf16).T

    def share_rows(ref, k, part):
        return send(ref.at[part, lanes(k)], ref.at[part, twin_lanes(k)], twin)

    theirs = rows((1 - core) * share, share)
    spread, traded = {}, {}

    def forward(k):
        straight[k].wait_recv()
        spread[k] = [
            send(xin.at[own, lanes(k)], xin.at[own, lanes(k)], along_x),
            send(xin.at[own, lanes(k)], xin.at[own, lanes(k)], along_y),
        ]

    def encode(k):
        if k == 1:
            straight[k].wait_recv()
        else:
            across[k].wait_recv()
            for copy in spread[k]:
                copy.wait_recv()

        @pl.loop(0, latent // step)
        def _(i):
            part = rows(i * step, step)
            pre = jnp.dot(enc_t[part, :], xin[:, lanes(k)], preferred_element_type=f32)
            value = jnp.maximum(pre + enc_wide[part, :], 0.0)
            active[part, slots(k)] = value
            latents[part, lanes(k)] = (value * value).astype(bf16)

    def trade(k):
        everything = rows(0, latent)
        traded[k] = [share_rows(latents, k, everything), share_rows(xin, k, theirs)]

    reduced = {}

    def decode(k, t):
        @pl.loop(0, 4)
        def _(q):
            product = jnp.dot(
                dec_t[t, rows(q * quarter, quarter), :],
                latents[:, lanes(k)],
                preferred_element_type=f32,
            ).astype(bf16)
            partial[k, t, q // 2, q % 2, 0] = product[:half]
            partial[k, t, q // 2, q % 2, 1] = product[half:]

        reduced[k, t] = [
            send(partial.at[k, t, :, 1 - low, 0], first_x.at[k, t], along_x),
            send(partial.at[k, t, 1 - high, :, 1], first_y.at[k, t], along_y),
        ]

    settled = {}

    def combine(k, t):
        for copy in reduced[k, t]:
            copy.wait_recv()
        next_y[k, t] = (
            partial[k, t, 1 - high, low, 0].astype(f32) + first_x[k, t, 1 - high].astype(f32)
        ).astype(bf16)
        next_x[k, t] = (
            partial[k, t, high, 1 - low, 1].astype(f32) + first_y[k, t, 1 - low].astype(f32)
        ).astype(bf16)
        settled[k, t] = [
            send(next_y.at[k, t], last_y.at[k, t], along_y),
            send(next_x.at[k, t], last_x.at[k, t], along_x),
        ]

    gathered, returned = {}, {}

    def judge(k, t):
        for copy in settled[k, t]:
            copy.wait_recv()
        if k and t == 0:
            flags[k].wait_recv()
            goals[k].wait_recv()
        scale = alive[0:1, slots(k)] * coef
        for h, (mine, late) in enumerate(
            ((first_x[k, t, high], last_y[k, t]), (first_y[k, t, low], last_x[k, t]))
        ):
            total = partial[k, t, high, low, h].astype(f32) + mine.astype(f32)
            total = (total + late.astype(f32)).astype(bf16).astype(f32)
            part = pl.ds(h * half, half)
            full = total + dec_wide[t, part, :]
            if k:
                back_out[k - 1, t, part, :] = full.astype(bf16)
            else:
                back_in[t, part, slots(0)] = full.astype(bf16)
            gap = full - goal[t, part, slots(k)].astype(f32)
            errors[t, rows(layer * quarter + h * half, half), lanes(k)] = (
                scale * gap
            ).astype(bf16)
        piece = errors.at[t, own, lanes(k)]
        gathered[k, t] = [send(piece, piece, along_x), send(piece, piece, along_y)]

    def give_back(k, t):
        returned[k, t] = send(back_out.at[k - 1, t], back_in.at[t, :, slots(k)], peers[k])

    relayed = {}

    def relay(k, t):
        for copy in gathered[k, t]:
            copy.wait_recv()
        from_x = errors.at[t, rows(beside_x * quarter, half), lanes(k)]
        from_y = errors.at[t, rows(beside_y * quarter + half, half), lanes(k)]
        relayed[k, t] = [send(from_x, from_x, along_y), send(from_y, from_y, along_x)]

    handed = {}

    def backward(k, t):
        for copy in relayed[k, t]:
            copy.wait_recv()
        handed[k, t] = share_rows(errors.at[t], k, theirs)

        @pl.loop(0, latent // step)
        def _(i):
            part = rows(i * step, step)
            value = jnp.dot(dec_in[t, part, :], errors[t, :, lanes(k)], preferred_element_type=f32)
            if t:
                value = value + grad_lat[part, :]
            if t < kinds - 1:
                grad_lat[part, :] = value
            else:
                grad_pre[part, lanes(k)] = (
                    value * (2.0 * active[part, slots(k)])
                ).astype(bf16)

        if t == kinds - 1:
            handed[k] = share_rows(grad_pre, k, rows(0, latent))

    third = share // 3
    final = 3

    def grow_dec(k, t):
        if t == 0:
            for copy in traded[k]:
                copy.wait_recv()
        handed[k, t].wait_recv()

        @pl.loop(0, 3)
        def _(j):
            part = pl.ds(pl.multiple_of(j * third, 128), third)
            value = rows_by_rows(
                latents[:, pair(k)], errors[t, rows(core * share + j * third, third), pair(k)]
            )
            if k:
                value = value + dec_sum[t, :, part]
            if k < final:
                dec_sum[t, :, part] = value
            else:
                dec_out[t, :, part] = value.astype(bf16)

    def grow_enc(k):
        handed[k].wait_recv()

        @pl.loop(0, 3)
        def _(j):
            part = rows(j * third, third)
            value = rows_by_rows(
                xin[rows(core * share + j * third, third), pair(k)], grad_pre[:, pair(k)]
            )
            if k:
                value = value + enc_sum[part, :]
            if k < final:
                enc_sum[part, :] = value
            else:
                enc_out[part, :] = value.astype(bf16)

    def each(stage, *key):
        for t in range(kinds):
            stage(*key, t)

    load_dec.wait()
    for t in range(kinds):

        @pl.loop(0, width // step)
        def _(i):
            part = rows(i * step, step)
            dec_t[t, part, :] = dec_in[t, :, part].T

        decode(0, t)

    @pl.loop(0, 3)
    def _(i):
        part = rows(i * wide, wide)
        moved = jnp.dot(
            place[2 * cap :, :], tok_in[:, part], preferred_element_type=f32
        ).astype(bf16)
        cells_far[part, :] = moved.T

    for m in (2, 3):
        straight[m] = send(cells_far.at[own, slots(m - 2)], xin.at[own, lanes(m)], peers[m])
    for m in (2, 3):
        across[m] = send(cells_far.at[other, slots(m - 2)], xin.at[other, lanes(m)], peers[m])
    trade(0)

    load_goal.wait()
    load_live.wait()
    load_b_dec.wait()
    live = jnp.broadcast_to(live_in[...].astype(f32).astype(bf16), (8, tok_rows))
    shown = rows_by_rows(live, place[...])
    alive[:, slots(0)] = shown[:, :cap]
    alive_out[...] = shown[:, cap:]
    for t in range(kinds):
        moved = rows_by_rows(goal_in[t], place[...]).astype(bf16)
        goal[t, :, slots(0)] = moved[:, :cap]
        goal_out[t] = moved[:, cap:]
        bias_pad[:, :quarter] = jnp.broadcast_to(b_dec_in[t : t + 1, :], (cap, quarter))
        dec_wide[t] = bias_pad[...].T[:quarter]
    for m in (1, 2, 3):
        flags[m] = send(alive_out.at[:, slots(m - 1)], alive.at[:, slots(m)], peers[m])
        goals[m] = send(goal_out.at[:, :, slots(m - 1)], goal.at[:, :, slots(m)], peers[m])

    bias_pad[:, :latent] = jnp.broadcast_to(b_enc_in[...], (cap, latent))
    enc_wide[...] = bias_pad[:, :latent].T

    @pl.loop(0, width // step)
    def _(i):
        part = rows(i * step, step)
        enc_t[:, part] = enc_in[part, :].T

    each(combine, 0)
    each(judge, 0)
    encode(1)
    each(decode, 1)
    trade(1)
    forward(2)
    each(relay, 0)
    forward(3)
    each(combine, 1)
    encode(2)
    each(decode, 2)
    trade(2)
    each(judge, 1)
    each(give_back, 1)
    each(combine, 2)
    each(backward, 0)
    each(relay, 1)
    encode(3)
    each(decode, 3)
    trade(3)
    each(judge, 2)
    each(give_back, 2)
    each(grow_dec, 0)
    grow_enc(0)
    each(combine, 3)
    each(backward, 1)
    each(relay, 2)
    for t in range(kinds):
        judge(3, t)
        give_back(3, t)
    ones = jnp.ones((8, cap), bf16)
    for t in range(kinds):
        err_sum[t] = sum(rows_by_rows(ones, errors[t, own, lanes(k)]) for k in range(4))
    err_swap = send(err_sum, err_came, twin)
    each(grow_dec, 1)
    grow_enc(1)
    err_swap.wait_recv()
    err_all[expert] = err_sum[...] + err_came[...]
    err_spread = [send(err_all.at[expert], err_all.at[expert], peers[m]) for m in (1, 2, 3)]
    backward(2, 0)
    relay(3, 0)
    grow_dec(2, 0)
    backward(2, 1)
    relay(3, 1)
    grow_dec(2, 1)
    grow_enc(2)
    backward(3, 0)
    grow_dec(3, 0)
    for k in (1, 2, 3):
        returned[k, 0].wait_recv()

    def restore(t):
        recon_out[t] = jnp.dot(
            back_in[t], place[...], preferred_element_type=f32
        ).astype(bf16)

    restore(0)
    backward(3, 1)
    grow_dec(3, 1)
    grow_enc(3)
    side = latent // 2
    bias_out[...] = rows_by_rows(
        jnp.ones((8, 8 * cap), bf16), grad_pre[rows(core * side, side), :]
    )[0:1]
    for t in range(1, kinds):
        for k in (1, 2, 3):
            returned[k, t].wait_recv()
        restore(t)
    for copy in err_spread:
        copy.wait_recv()
    for t in range(kinds):
        total = err_all[0, t] + err_all[1, t] + err_all[2, t] + err_all[3, t]
        bdec_out[t : t + 1, :] = total[0:1]

    for copy in sends:
        copy.wait_send()


def store_kernel(*refs):
    sources, results, sem = refs[:5], refs[5:10], refs[10]
    copies = [
        pltpu.make_async_copy(source, result, sem.at[number])
        for number, (source, result) in enumerate(zip(sources, results))
    ]
    for copy in copies:
        copy.start()
    for copy in copies:
        copy.wait()


def local(tokens, expert_ids, slot_ids, live_mask, w_enc, b_enc, w_dec, b_dec, targets):
    f32, bf16 = jnp.float32, jnp.bfloat16
    n_expert = lax.axis_size("expert")
    n_layer = lax.axis_size("layer")
    assert lax.axis_size("dp") == 2
    if n_expert != 4 or n_layer != 4:
        return plain(
            tokens, expert_ids, slot_ids, live_mask, w_enc, b_enc, w_dec, b_dec, targets
        )
    tok_rows, width = tokens.shape
    cap = 2 * tok_rows // n_expert
    count = n_expert * cap
    quarter, share = width // 4, width // 2
    half = quarter // 2
    padded = -(-quarter // 128) * 128
    latent = w_enc.shape[2]
    kinds = w_dec.shape[0]
    rest = count - cap

    vmem = pl.BlockSpec(memory_space=pltpu.VMEM)
    hbm = pl.BlockSpec(memory_space=pl.ANY)
    scratch = [
        ((1, tok_rows), jnp.int32),
        ((1, tok_rows), jnp.int32),
        ((1, tok_rows), jnp.int32),
        ((1, latent), f32),
        ((kinds, quarter), f32),
        ((tok_rows, width), bf16),
        ((cap, width), bf16),
        ((kinds, quarter, tok_rows), bf16),
        ((count, tok_rows), bf16),
        ((cap, max(padded, latent)), f32),
        ((latent, cap), f32),
        ((kinds, quarter, cap), f32),
        ((width, cap), bf16),
        ((width, rest - cap), bf16),
        ((kinds, quarter, rest), bf16),
        ((8, rest), f32),
        ((width, latent), bf16),
        ((latent, width), bf16),
        ((kinds, latent, width), bf16),
        ((kinds, width, latent), bf16),
        ((width, 2 * count), bf16),
        ((kinds, quarter, count), bf16),
        ((8, count), f32),
        ((latent, 2 * count), bf16),
        ((latent, count), f32),
        ((latent, cap), f32),
        ((latent, 2 * count), bf16),
        ((4, kinds, 2, 2, 2, half, cap), bf16),
        ((4, kinds, 2, half, cap), bf16),
        ((4, kinds, 2, half, cap), bf16),
        ((4, kinds, half, cap), bf16),
        ((4, kinds, half, cap), bf16),
        ((4, kinds, half, cap), bf16),
        ((4, kinds, half, cap), bf16),
        ((kinds, width, 2 * count), bf16),
        ((3, kinds, quarter, cap), bf16),
        ((kinds, quarter, count), bf16),
        ((kinds, latent, share), f32),
        ((share, latent), f32),
        ((kinds, 8, quarter), f32),
        ((kinds, 8, quarter), f32),
        ((4, kinds, 8, quarter), f32),
    ]
    results = [
        ((kinds, quarter, tok_rows), bf16),
        ((share, latent), bf16),
        ((1, latent // 2), f32),
        ((kinds, latent, share), bf16),
        ((kinds, quarter), f32),
    ]
    made = pl.pallas_call(
        step_kernel,
        out_shape=tuple(pltpu.VMEM(shape, dtype) for shape, dtype in results),
        in_specs=[hbm] * 9,
        out_specs=(vmem,) * 5,
        scratch_shapes=[pltpu.VMEM(shape, dtype) for shape, dtype in scratch]
        + [
            pltpu.SemaphoreType.DMA((COPIES,)),
            pltpu.SemaphoreType.DMA((COPIES,)),
            pltpu.SemaphoreType.DMA((9,)),
        ],
        compiler_params=pltpu.CompilerParams(
            collective_id=0, has_side_effects=True, vmem_limit_bytes=60 * 10**6
        ),
        name="step",
    )(
        expert_ids[None],
        slot_ids[None],
        live_mask[None],
        b_enc,
        b_dec,
        tokens,
        jnp.swapaxes(targets, 1, 2),
        w_enc[0],
        w_dec[:, 0],
    )
    recon, enc, bias, dec, bdec = pl.pallas_call(
        store_kernel,
        out_shape=tuple(jax.ShapeDtypeStruct(shape, dtype) for shape, dtype in results),
        in_specs=[vmem] * 5,
        out_specs=(hbm,) * 5,
        scratch_shapes=[pltpu.SemaphoreType.DMA((5,))],
        compiler_params=pltpu.CompilerParams(vmem_limit_bytes=2**20),
        name="store",
    )(*[pltpu.with_memory_space_constraint(value, pltpu.VMEM) for value in made])
    return (jnp.swapaxes(recon, 1, 2), enc[None], bias, dec[:, None], bdec)


def solution(mesh):
    placed = (
        P(("expert", "dp"), None),
        P(("expert", "dp")),
        P(("expert", "dp")),
        P(("expert", "dp")),
        P("expert", None, "layer"),
        P("expert", "layer"),
        P(None, "expert", "layer", None),
        P(None, "layer"),
        P(None, ("expert", "dp"), "layer"),
    )
    return jax.shard_map(
        local,
        mesh=mesh,
        in_specs=placed,
        out_specs=(
            P(None, ("expert", "dp"), "layer"),
            P("expert", "dp", "layer"),
            P("expert", ("layer", "dp")),
            P(None, "expert", "layer", "dp"),
            P(None, "layer"),
        ),
        check_vma=False,
    )
```

```python
import math

import jax
import jax.numpy as jnp
from jax import lax
from jax.experimental import pallas as pl
from jax.experimental.pallas import tpu as pltpu
from jax.sharding import PartitionSpec as P


def swap(values, mask, axis="layer"):
    size = lax.axis_size(axis)
    return lax.ppermute(values, axis, [(i, i ^ mask) for i in range(size)])


def exchange_experts(values):
    size = lax.axis_size("expert")
    if size != 4:
        return lax.all_to_all(values, "expert", split_axis=1, concat_axis=1, tiled=True)
    width = values.shape[1] // size
    blocks = [values[:, k * width : (k + 1) * width] for k in range(size)]
    for mask in (2, 3, 1):
        blocks[mask] = swap(blocks[mask], mask, "expert")
    return jnp.concatenate(blocks, axis=1)


def sum_all(values, axes):
    for axis in axes:
        size = lax.axis_size(axis)
        if size & (size - 1):
            values = lax.psum(values, axis)
            continue
        mask = 1
        while mask < size:
            values = values + swap(values, mask, axis)
            mask *= 2
    return values


def share_sum(product, rows, fills):
    depth = rows.shape[0] // 2
    me = lax.axis_index("dp")
    sent = product(lax.dynamic_slice_in_dim(rows, (1 - me) * depth, depth, 0))
    came = swap(sent.astype(fills), 1, "dp")
    own = product(lax.dynamic_slice_in_dim(rows, me * depth, depth, 0))
    return own + came.astype(jnp.float32)


def gather_layers(piece, beside=None):
    size = lax.axis_size("layer")
    if size != 4 or piece.shape[0] % 2:
        return lax.all_gather(piece, "layer", axis=0, tiled=True), beside
    me = lax.axis_index("layer")
    depth = piece.shape[0]
    half = depth // 2
    near = swap(piece, 1)
    far = swap(piece, 2)
    if beside is not None:
        near, far, beside = lax.optimization_barrier((near, far, beside))
    first = swap(far[:half], 1)
    second = swap(near[half:], 2)
    whole = jnp.zeros((size * depth,) + piece.shape[1:], piece.dtype)
    for offset, value in (
        (me * depth, piece),
        ((me ^ 1) * depth, near),
        ((me ^ 2) * depth, far),
        ((me ^ 3) * depth, first),
        ((me ^ 3) * depth + half, second),
    ):
        whole = lax.dynamic_update_slice_in_dim(whole, value, offset, 0)
    return whole, beside


def scatter_sum(values):
    size = lax.axis_size("layer")
    depth = values.shape[0] // size
    if size != 4 or depth % 2:
        return lax.psum_scatter(values, "layer", scatter_dimension=0, tiled=True)
    f32 = jnp.float32
    me = lax.axis_index("layer")
    low, high = me % 2, me // 2
    pieces = values.reshape((2, 2, 2, depth // 2) + values.shape[1:])

    def pick(array, index, axis):
        return lax.dynamic_index_in_dim(array, index, axis, keepdims=False)

    one, two = pieces[:, :, 0], pieces[:, :, 1]
    one_in = swap(pick(one, 1 - low, 1), 1)
    two_in = swap(pick(two, 1 - high, 0), 2)
    one_sum = pick(one, low, 1).astype(f32) + one_in.astype(f32)
    two_sum = pick(two, high, 0).astype(f32) + two_in.astype(f32)
    one_last = swap(pick(one_sum, 1 - high, 0).astype(values.dtype), 2)
    two_last = swap(pick(two_sum, 1 - low, 0).astype(values.dtype), 1)
    return jnp.concatenate(
        [
            (pick(one_sum, high, 0) + one_last.astype(f32)).astype(values.dtype),
            (pick(two_sum, low, 0) + two_last.astype(f32)).astype(values.dtype),
        ]
    )


def plain(tokens, expert_ids, slot_ids, live_mask, w_enc, b_enc, w_dec, b_dec, targets):
    f32, bf16 = jnp.float32, jnp.bfloat16
    n_expert = lax.axis_size("expert")
    n_layer = lax.axis_size("layer")
    assert lax.axis_size("dp") == 2
    tok_rows, model_width = tokens.shape
    capacity = 2 * tok_rows // n_expert
    total_cells = n_expert * capacity
    offset = lax.axis_index("expert") if n_expert == 4 else 0
    cell_index = (expert_ids ^ offset) * capacity + slot_ids
    quarter = model_width // n_layer
    targets_count = w_dec.shape[0]
    enc_weight = w_enc[0]
    place = (
        lax.broadcasted_iota(jnp.int32, (total_cells, tok_rows), 0) == cell_index[None, :]
    ).astype(bf16)

    cells = lax.dot_general(
        tokens, place, (((0,), (1,)), ((), ())), preferred_element_type=f32
    ).astype(bf16)
    own = lax.dynamic_slice_in_dim(cells, lax.axis_index("layer") * quarter, quarter, 0)
    arrived_part = exchange_experts(own)
    arrived, _ = gather_layers(arrived_part)
    pre_act = jnp.einsum("dr,dl->rl", arrived, enc_weight, preferred_element_type=f32)
    pre_act = pre_act + b_enc[0][None, :]
    active = jnp.maximum(pre_act, 0.0)
    latents = (active * active).astype(bf16)

    coef = 2.0 / math.sqrt(tok_rows)
    live_wide = live_mask.astype(f32)
    partials = [
        jnp.einsum("ld,rl->dr", w_dec[t, 0], latents, preferred_element_type=f32).astype(bf16)
        for t in range(targets_count)
    ]
    summed = [scatter_sum(p) for p in partials]
    recons, errors, parts = [], [], []
    for t in range(targets_count):
        returned = exchange_experts(summed[t])
        recon_sum = jnp.einsum("dr,ri->di", returned, place, preferred_element_type=f32)
        recon_full = recon_sum + b_dec[t][:, None]
        recons.append(recon_full.astype(bf16).T)
        error = (
            coef * live_wide[None, :] * (recon_full - targets[t].T.astype(f32))
        ).astype(bf16)
        errors.append(jnp.sum(error.astype(f32), axis=1))
        outgoing = jnp.einsum(
            "di,ri->dr", error, place, preferred_element_type=f32
        ).astype(bf16)
        parts.append(exchange_experts(outgoing))
    recon = jnp.stack(recons)
    grad_b_dec = sum_all(jnp.stack(errors), ("dp", "expert"))
    beside = parts[1:] + [None]
    segments = []
    for t in range(targets_count):
        segment, beside[t] = gather_layers(parts[t], beside[t])
        if t + 1 < targets_count:
            parts[t + 1] = beside[t]
        segments.append(segment)

    grad_lat = sum(
        jnp.einsum("dr,ld->rl", segments[t], w_dec[t, 0], preferred_element_type=f32)
        for t in range(targets_count)
    )
    dec_parts = [
        share_sum(
            lambda rows: jnp.einsum("dr,rl->dl", rows, latents, preferred_element_type=f32),
            segments[t],
            bf16,
        ).astype(bf16)
        for t in range(targets_count)
    ]
    grad_pre = (grad_lat * (2.0 * active)).astype(bf16)
    enc_share = share_sum(
        lambda rows: jnp.einsum("dr,rl->dl", rows, grad_pre, preferred_element_type=f32),
        arrived,
        bf16,
    ).astype(bf16)
    grad_bias = jnp.sum(lax.optimization_barrier(grad_pre).astype(f32), axis=0)
    bias_share = share_sum(lambda rows: rows, grad_bias, f32)
    dec_share = jnp.stack([part.T for part in dec_parts])[:, None]
    return (recon, enc_share[None], bias_share[None], dec_share, grad_b_dec)


MESH = pl.DeviceIdType.MESH
COPIES = 128


def rows_by_rows(left, right):
    return lax.dot_general(
        left, right, (((1,), (1,)), ((), ())), preferred_element_type=jnp.float32
    )


def step_kernel(
    expert_ids,
    slot_ids,
    live_mask,
    b_enc,
    b_dec,
    tokens,
    targets,
    w_enc,
    w_dec,
    recon_out,
    enc_out,
    bias_out,
    dec_out,
    bdec_out,
    ids_in,
    slot_in,
    live_in,
    b_enc_in,
    b_dec_in,
    tok_in,
    x_rows,
    goal_in,
    place,
    bias_pad,
    enc_wide,
    dec_wide,
    cells_near,
    cells_far,
    goal_out,
    alive_out,
    enc_in,
    enc_t,
    dec_in,
    dec_t,
    xin,
    goal,
    alive,
    latents,
    active,
    grad_lat,
    grad_pre,
    partial,
    first_x,
    first_y,
    next_x,
    next_y,
    last_x,
    last_y,
    errors,
    back_out,
    back_in,
    dec_sum,
    enc_sum,
    err_sum,
    err_came,
    err_all,
    send_sem,
    recv_sem,
    load_sem,
):
    f32, bf16 = jnp.float32, jnp.bfloat16
    layer = lax.axis_index("layer")
    expert = lax.axis_index("expert")
    core = lax.axis_index("dp")
    low, high = layer % 2, layer // 2
    beside_x = high * 2 + 1 - low
    beside_y = (1 - high) * 2 + low
    facing = 3 - layer
    along_x, along_y = {"layer": beside_x}, {"layer": beside_y}
    peers = {
        1: {"expert": expert + 1 - 2 * (expert % 2)},
        2: {"expert": (expert + 2) % 4},
        3: {"expert": 3 - expert},
    }
    twin = {"dp": 1 - core}

    tok_rows, width = tok_in.shape
    kinds = goal_in.shape[0]
    latent = enc_in.shape[1]
    count = place.shape[0]
    quarter = width // 4
    half = quarter // 2
    share = width // 2
    cap = count // 4
    coef = 2.0 / math.sqrt(tok_rows)

    def lanes(block):
        return pl.ds(block * 2 * cap, cap)

    def twin_lanes(block):
        return pl.ds(block * 2 * cap + cap, cap)

    def pair(block):
        return pl.ds(block * 2 * cap, 2 * cap)

    def slots(block):
        return pl.ds(block * cap, cap)

    def rows(start, size):
        return pl.ds(pl.multiple_of(start, 16), size)

    sends = []

    def send(source, target, device):
        number = len(sends)
        copy = pltpu.make_async_remote_copy(
            src_ref=source,
            dst_ref=target,
            send_sem=send_sem.at[number],
            recv_sem=recv_sem.at[number],
            device_id=device,
            device_id_type=MESH,
        )
        copy.start()
        sends.append(copy)
        return copy

    barrier = pltpu.get_barrier_semaphore()
    partners = [peers[1], peers[2], peers[3], along_x, along_y, twin]
    for partner in partners:
        pl.semaphore_signal(barrier, inc=1, device_id=partner, device_id_type=MESH)
    loads = [
        pltpu.make_async_copy(source, target, load_sem.at[number])
        for number, (source, target) in enumerate(
            [
                (expert_ids, ids_in),
                (slot_ids, slot_in),
                (tokens, tok_in),
                (b_enc, b_enc_in),
                (w_enc, enc_in),
                (w_dec, dec_in),
                (b_dec, b_dec_in),
                (live_mask, live_in),
                (targets, goal_in),
            ]
        )
    ]
    load_ids, load_slots, load_tokens, load_b_enc, load_enc = loads[:5]
    load_dec, load_b_dec, load_live, load_goal = loads[5:]
    for load in loads:
        load.start()

    own = rows(layer * quarter, quarter)
    other = rows(facing * quarter, quarter)
    step = 256
    wide = width // 3

    load_ids.wait()
    load_slots.wait()
    cell = (ids_in[...] ^ expert) * cap + slot_in[...]
    marks = lax.broadcasted_iota(jnp.int32, (count, tok_rows), 0) == cell
    place[...] = jnp.where(marks, 1.0, 0.0).astype(bf16)
    load_tokens.wait()

    @pl.loop(0, 3)
    def _(i):
        part = rows(i * wide, wide)
        moved = jnp.dot(
            place[: 2 * cap, :], tok_in[:, part], preferred_element_type=f32
        ).astype(bf16)
        x_rows[:, part] = moved[:cap]
        turned = moved.T
        xin[part, lanes(0)] = turned[:, :cap]
        cells_near[part, :] = turned[:, cap:]

    straight, across, flags, goals = {}, {}, {}, {}
    pl.semaphore_wait(barrier, len(partners))
    straight[1] = send(cells_near, xin.at[:, lanes(1)], peers[1])
    load_b_enc.wait()
    load_enc.wait()

    @pl.loop(0, latent // step)
    def _(i):
        part = rows(i * step, step)
        pre = jnp.dot(x_rows[...], enc_in[:, part], preferred_element_type=f32)
        value = jnp.maximum(pre + b_enc_in[:, part], 0.0)
        active[part, slots(0)] = value.T
        latents[part, lanes(0)] = (value * value).astype(bf16).T

    def share_rows(ref, k, part):
        return send(ref.at[part, lanes(k)], ref.at[part, twin_lanes(k)], twin)

    theirs = rows((1 - core) * share, share)
    spread, traded = {}, {}

    def forward(k):
        straight[k].wait_recv()
        spread[k] = [
            send(xin.at[own, lanes(k)], xin.at[own, lanes(k)], along_x),
            send(xin.at[own, lanes(k)], xin.at[own, lanes(k)], along_y),
        ]

    def encode(k):
        if k == 1:
            straight[k].wait_recv()
        else:
            across[k].wait_recv()
            for copy in spread[k]:
                copy.wait_recv()

        @pl.loop(0, latent // step)
        def _(i):
            part = rows(i * step, step)
            pre = jnp.dot(enc_t[part, :], xin[:, lanes(k)], preferred_element_type=f32)
            value = jnp.maximum(pre + enc_wide[part, :], 0.0)
            active[part, slots(k)] = value
            latents[part, lanes(k)] = (value * value).astype(bf16)

    def trade(k):
        everything = rows(0, latent)
        traded[k] = [share_rows(latents, k, everything), share_rows(xin, k, theirs)]

    reduced = {}

    def decode(k, t):
        @pl.loop(0, 4)
        def _(q):
            product = jnp.dot(
                dec_t[t, rows(q * quarter, quarter), :],
                latents[:, lanes(k)],
                preferred_element_type=f32,
            ).astype(bf16)
            partial[k, t, q // 2, q % 2, 0] = product[:half]
            partial[k, t, q // 2, q % 2, 1] = product[half:]

        reduced[k, t] = [
            send(partial.at[k, t, :, 1 - low, 0], first_x.at[k, t], along_x),
            send(partial.at[k, t, 1 - high, :, 1], first_y.at[k, t], along_y),
        ]

    settled = {}

    def combine(k, t):
        for copy in reduced[k, t]:
            copy.wait_recv()
        next_y[k, t] = (
            partial[k, t, 1 - high, low, 0].astype(f32) + first_x[k, t, 1 - high].astype(f32)
        ).astype(bf16)
        next_x[k, t] = (
            partial[k, t, high, 1 - low, 1].astype(f32) + first_y[k, t, 1 - low].astype(f32)
        ).astype(bf16)
        settled[k, t] = [
            send(next_y.at[k, t], last_y.at[k, t], along_y),
            send(next_x.at[k, t], last_x.at[k, t], along_x),
        ]

    gathered, returned = {}, {}

    def judge(k, t):
        for copy in settled[k, t]:
            copy.wait_recv()
        if k and t == 0:
            flags[k].wait_recv()
            goals[k].wait_recv()
        scale = alive[0:1, slots(k)] * coef
        for h, (mine, late) in enumerate(
            ((first_x[k, t, high], last_y[k, t]), (first_y[k, t, low], last_x[k, t]))
        ):
            total = partial[k, t, high, low, h].astype(f32) + mine.astype(f32)
            total = (total + late.astype(f32)).astype(bf16).astype(f32)
            part = pl.ds(h * half, half)
            full = total + dec_wide[t, part, :]
            if k:
                back_out[k - 1, t, part, :] = full.astype(bf16)
            else:
                back_in[t, part, slots(0)] = full.astype(bf16)
            gap = full - goal[t, part, slots(k)].astype(f32)
            errors[t, rows(layer * quarter + h * half, half), lanes(k)] = (
                scale * gap
            ).astype(bf16)
        piece = errors.at[t, own, lanes(k)]
        gathered[k, t] = [send(piece, piece, along_x), send(piece, piece, along_y)]

    def give_back(k, t):
        returned[k, t] = send(back_out.at[k - 1, t], back_in.at[t, :, slots(k)], peers[k])

    relayed = {}

    def relay(k, t):
        for copy in gathered[k, t]:
            copy.wait_recv()
        from_x = errors.at[t, rows(beside_x * quarter, half), lanes(k)]
        from_y = errors.at[t, rows(beside_y * quarter + half, half), lanes(k)]
        relayed[k, t] = [send(from_x, from_x, along_y), send(from_y, from_y, along_x)]

    handed = {}

    def backward(k, t):
        for copy in relayed[k, t]:
            copy.wait_recv()
        handed[k, t] = share_rows(errors.at[t], k, theirs)

        @pl.loop(0, latent // step)
        def _(i):
            part = rows(i * step, step)
            value = jnp.dot(dec_in[t, part, :], errors[t, :, lanes(k)], preferred_element_type=f32)
            if t:
                value = value + grad_lat[part, :]
            if t < kinds - 1:
                grad_lat[part, :] = value
            else:
                grad_pre[part, lanes(k)] = (
                    value * (2.0 * active[part, slots(k)])
                ).astype(bf16)

        if t == kinds - 1:
            handed[k] = share_rows(grad_pre, k, rows(0, latent))

    third = share // 3
    final = 3

    def grow_dec(k, t):
        if t == 0:
            for copy in traded[k]:
                copy.wait_recv()
        handed[k, t].wait_recv()

        @pl.loop(0, 3)
        def _(j):
            part = pl.ds(pl.multiple_of(j * third, 128), third)
            value = rows_by_rows(
                latents[:, pair(k)], errors[t, rows(core * share + j * third, third), pair(k)]
            )
            if k:
                value = value + dec_sum[t, :, part]
            if k < final:
                dec_sum[t, :, part] = value
            else:
                dec_out[t, :, part] = value.astype(bf16)

    def grow_enc(k):
        handed[k].wait_recv()

        @pl.loop(0, 3)
        def _(j):
            part = rows(j * third, third)
            value = rows_by_rows(
                xin[rows(core * share + j * third, third), pair(k)], grad_pre[:, pair(k)]
            )
            if k:
                value = value + enc_sum[part, :]
            if k < final:
                enc_sum[part, :] = value
            else:
                enc_out[part, :] = value.astype(bf16)

    def each(stage, *key):
        for t in range(kinds):
            stage(*key, t)

    load_dec.wait()
    for t in range(kinds):

        @pl.loop(0, width // step)
        def _(i):
            part = rows(i * step, step)
            dec_t[t, part, :] = dec_in[t, :, part].T

        decode(0, t)

    @pl.loop(0, 3)
    def _(i):
        part = rows(i * wide, wide)
        moved = jnp.dot(
            place[2 * cap :, :], tok_in[:, part], preferred_element_type=f32
        ).astype(bf16)
        cells_far[part, :] = moved.T

    for m in (2, 3):
        straight[m] = send(cells_far.at[own, slots(m - 2)], xin.at[own, lanes(m)], peers[m])
    for m in (2, 3):
        across[m] = send(cells_far.at[other, slots(m - 2)], xin.at[other, lanes(m)], peers[m])
    trade(0)

    load_goal.wait()
    load_live.wait()
    load_b_dec.wait()
    live = jnp.broadcast_to(live_in[...].astype(f32).astype(bf16), (8, tok_rows))
    shown = rows_by_rows(live, place[...])
    alive[:, slots(0)] = shown[:, :cap]
    alive_out[...] = shown[:, cap:]
    for t in range(kinds):
        moved = rows_by_rows(goal_in[t], place[...]).astype(bf16)
        goal[t, :, slots(0)] = moved[:, :cap]
        goal_out[t] = moved[:, cap:]
        bias_pad[:, :quarter] = jnp.broadcast_to(b_dec_in[t : t + 1, :], (cap, quarter))
        dec_wide[t] = bias_pad[...].T[:quarter]
    for m in (1, 2, 3):
        flags[m] = send(alive_out.at[:, slots(m - 1)], alive.at[:, slots(m)], peers[m])
        goals[m] = send(goal_out.at[:, :, slots(m - 1)], goal.at[:, :, slots(m)], peers[m])

    bias_pad[:, :latent] = jnp.broadcast_to(b_enc_in[...], (cap, latent))
    enc_wide[...] = bias_pad[:, :latent].T

    @pl.loop(0, width // step)
    def _(i):
        part = rows(i * step, step)
        enc_t[:, part] = enc_in[part, :].T

    each(combine, 0)
    each(judge, 0)
    encode(1)
    each(decode, 1)
    trade(1)
    forward(2)
    each(relay, 0)
    forward(3)
    each(combine, 1)
    encode(2)
    each(decode, 2)
    trade(2)
    each(judge, 1)
    each(give_back, 1)
    each(combine, 2)
    each(backward, 0)
    each(relay, 1)
    encode(3)
    each(decode, 3)
    trade(3)
    each(judge, 2)
    each(give_back, 2)
    each(grow_dec, 0)
    grow_enc(0)
    each(combine, 3)
    each(backward, 1)
    each(relay, 2)
    for t in range(kinds):
        judge(3, t)
        give_back(3, t)
    ones = jnp.ones((8, cap), bf16)
    for t in range(kinds):
        err_sum[t] = sum(rows_by_rows(ones, errors[t, own, lanes(k)]) for k in range(4))
    err_swap = send(err_sum, err_came, twin)
    each(grow_dec, 1)
    grow_enc(1)
    err_swap.wait_recv()
    err_all[expert] = err_sum[...] + err_came[...]
    err_spread = [send(err_all.at[expert], err_all.at[expert], peers[m]) for m in (1, 2, 3)]
    backward(2, 0)
    relay(3, 0)
    grow_dec(2, 0)
    backward(2, 1)
    relay(3, 1)
    grow_dec(2, 1)
    backward(3, 0)
    grow_enc(2)
    grow_dec(3, 0)
    for k in (1, 2, 3):
        returned[k, 0].wait_recv()

    def restore(t):
        recon_out[t] = jnp.dot(
            back_in[t], place[...], preferred_element_type=f32
        ).astype(bf16)

    restore(0)
    backward(3, 1)
    grow_dec(3, 1)
    grow_enc(3)
    side = latent // 2
    bias_out[...] = rows_by_rows(
        jnp.ones((8, 8 * cap), bf16), grad_pre[rows(core * side, side), :]
    )[0:1]
    for t in range(1, kinds):
        for k in (1, 2, 3):
            returned[k, t].wait_recv()
        restore(t)
    for copy in err_spread:
        copy.wait_recv()
    for t in range(kinds):
        total = err_all[0, t] + err_all[1, t] + err_all[2, t] + err_all[3, t]
        bdec_out[t : t + 1, :] = total[0:1]

    for copy in sends:
        copy.wait_send()


def store_kernel(*refs):
    sources, results, sem = refs[:5], refs[5:10], refs[10]
    copies = [
        pltpu.make_async_copy(source, result, sem.at[number])
        for number, (source, result) in enumerate(zip(sources, results))
    ]
    for copy in copies:
        copy.start()
    for copy in copies:
        copy.wait()


def local(tokens, expert_ids, slot_ids, live_mask, w_enc, b_enc, w_dec, b_dec, targets):
    f32, bf16 = jnp.float32, jnp.bfloat16
    n_expert = lax.axis_size("expert")
    n_layer = lax.axis_size("layer")
    assert lax.axis_size("dp") == 2
    if n_expert != 4 or n_layer != 4:
        return plain(
            tokens, expert_ids, slot_ids, live_mask, w_enc, b_enc, w_dec, b_dec, targets
        )
    tok_rows, width = tokens.shape
    cap = 2 * tok_rows // n_expert
    count = n_expert * cap
    quarter, share = width // 4, width // 2
    half = quarter // 2
    padded = -(-quarter // 128) * 128
    latent = w_enc.shape[2]
    kinds = w_dec.shape[0]
    rest = count - cap

    vmem = pl.BlockSpec(memory_space=pltpu.VMEM)
    hbm = pl.BlockSpec(memory_space=pl.ANY)
    scratch = [
        ((1, tok_rows), jnp.int32),
        ((1, tok_rows), jnp.int32),
        ((1, tok_rows), jnp.int32),
        ((1, latent), f32),
        ((kinds, quarter), f32),
        ((tok_rows, width), bf16),
        ((cap, width), bf16),
        ((kinds, quarter, tok_rows), bf16),
        ((count, tok_rows), bf16),
        ((cap, max(padded, latent)), f32),
        ((latent, cap), f32),
        ((kinds, quarter, cap), f32),
        ((width, cap), bf16),
        ((width, rest - cap), bf16),
        ((kinds, quarter, rest), bf16),
        ((8, rest), f32),
        ((width, latent), bf16),
        ((latent, width), bf16),
        ((kinds, latent, width), bf16),
        ((kinds, width, latent), bf16),
        ((width, 2 * count), bf16),
        ((kinds, quarter, count), bf16),
        ((8, count), f32),
        ((latent, 2 * count), bf16),
        ((latent, count), f32),
        ((latent, cap), f32),
        ((latent, 2 * count), bf16),
        ((4, kinds, 2, 2, 2, half, cap), bf16),
        ((4, kinds, 2, half, cap), bf16),
        ((4, kinds, 2, half, cap), bf16),
        ((4, kinds, half, cap), bf16),
        ((4, kinds, half, cap), bf16),
        ((4, kinds, half, cap), bf16),
        ((4, kinds, half, cap), bf16),
        ((kinds, width, 2 * count), bf16),
        ((3, kinds, quarter, cap), bf16),
        ((kinds, quarter, count), bf16),
        ((kinds, latent, share), f32),
        ((share, latent), f32),
        ((kinds, 8, quarter), f32),
        ((kinds, 8, quarter), f32),
        ((4, kinds, 8, quarter), f32),
    ]
    results = [
        ((kinds, quarter, tok_rows), bf16),
        ((share, latent), bf16),
        ((1, latent // 2), f32),
        ((kinds, latent, share), bf16),
        ((kinds, quarter), f32),
    ]
    made = pl.pallas_call(
        step_kernel,
        out_shape=tuple(pltpu.VMEM(shape, dtype) for shape, dtype in results),
        in_specs=[hbm] * 9,
        out_specs=(vmem,) * 5,
        scratch_shapes=[pltpu.VMEM(shape, dtype) for shape, dtype in scratch]
        + [
            pltpu.SemaphoreType.DMA((COPIES,)),
            pltpu.SemaphoreType.DMA((COPIES,)),
            pltpu.SemaphoreType.DMA((9,)),
        ],
        compiler_params=pltpu.CompilerParams(
            collective_id=0, has_side_effects=True, vmem_limit_bytes=60 * 10**6
        ),
        name="step",
    )(
        expert_ids[None],
        slot_ids[None],
        live_mask[None],
        b_enc,
        b_dec,
        tokens,
        jnp.swapaxes(targets, 1, 2),
        w_enc[0],
        w_dec[:, 0],
    )
    recon, enc, bias, dec, bdec = pl.pallas_call(
        store_kernel,
        out_shape=tuple(jax.ShapeDtypeStruct(shape, dtype) for shape, dtype in results),
        in_specs=[vmem] * 5,
        out_specs=(hbm,) * 5,
        scratch_shapes=[pltpu.SemaphoreType.DMA((5,))],
        compiler_params=pltpu.CompilerParams(vmem_limit_bytes=2**20),
        name="store",
    )(*[pltpu.with_memory_space_constraint(value, pltpu.VMEM) for value in made])
    return (jnp.swapaxes(recon, 1, 2), enc[None], bias, dec[:, None], bdec)


def solution(mesh):
    placed = (
        P(("expert", "dp"), None),
        P(("expert", "dp")),
        P(("expert", "dp")),
        P(("expert", "dp")),
        P("expert", None, "layer"),
        P("expert", "layer"),
        P(None, "expert", "layer", None),
        P(None, "layer"),
        P(None, ("expert", "dp"), "layer"),
    )
    return jax.shard_map(
        local,
        mesh=mesh,
        in_specs=placed,
        out_specs=(
            P(None, ("expert", "dp"), "layer"),
            P("expert", "dp", "layer"),
            P("expert", ("layer", "dp")),
            P(None, "expert", "layer", "dp"),
            P(None, "layer"),
        ),
        check_vma=False,
    )
```
